256 devices in a mesh: dp: 16 (over x, y), tensor: 16 (over z, core).
Axes of the slice: x: 4, y: 4, z: 8, core: 2. Of those that a mesh axis runs over, the one named last changes fastest.
Arguments:
- out_grad: bfloat16 [12288, 8192], P('dp', 'tensor'), may hold values from -6 to 6
- block_input: bfloat16 [12288, 8192], P('dp', 'tensor'), may hold values from -6 to 6
- gate_pre: bfloat16 [12288, 14336], P('dp', 'tensor'), may hold values from -8 to 8
- up_pre: bfloat16 [12288, 14336], P('dp', 'tensor'), may hold values from -6 to 6
- down_weight: bfloat16 [14336, 8192], P('tensor', 'dp'), may hold values from -0.046875 to 0.046875
- gate_in: bfloat16 [48, 16, 8192], P(None, None, 'tensor'), may hold values from -0.0625 to 0.0625
- gate_adapter_output_maps: bfloat16 [48, 16, 14336], P(None, None, 'tensor'), may hold values from -0.046875 to 0.046875
- up_in: bfloat16 [48, 16, 8192], P(None, None, 'tensor'), may hold values from -0.0625 to 0.0625
- up_adapter_output_maps: bfloat16 [48, 16, 14336], P(None, None, 'tensor'), may hold values from -0.046875 to 0.046875
- down_in: bfloat16 [48, 16, 14336], P(None, None, 'tensor'), may hold values from -0.046875 to 0.046875
- down_out: bfloat16 [48, 16, 8192], P(None, None, 'tensor'), may hold values from -0.0625 to 0.0625
- block_adapter: int32 [96], replicated, may hold values from 0 to 47, as said below
- owned_ids: int32 [48], replicated, may hold values from 0 to 47, as said below
Outputs:
- input_grad: bfloat16 [12288, 8192], P('dp', 'tensor')
- grad_gate_in: float32 [48, 16, 8192], P('dp', None, 'tensor')
- grad_gate_out: float32 [48, 16, 14336], P('dp', None, 'tensor')
- grad_up_in: float32 [48, 16, 8192], P('dp', None, 'tensor')
- grad_up_out: float32 [48, 16, 14336], P('dp', None, 'tensor')
- grad_down_in: float32 [48, 16, 14336], P('dp', None, 'tensor')
- grad_down_out: float32 [48, 16, 8192], P('dp', None, 'tensor')
The draws below stay inside these ranges and needn't reach their ends.
Inputs may be any that keep to these rules, and one draw needn't show every extreme that they name: `block_adapter`: replica q (blocks q * 6 to q * 6 + 5) owns the adapters owned_ids[q * 3] to owned_ids[q * 3 + 2]. Among the 6 blocks of one replica, at most 1 names an adapter of any one owner; in every draw each replica has some owner that it names exactly once. `owned_ids`: each adapter appears once.
All inputs are finite; a program needn't handle non-finite values.
Results may differ from the reference program's by a relative error of at most 0.0058.
Values may be sent and summed in bfloat16 or wider, within the bound.
A program may use at most 128 MiB of HBM per device.

```python
import jax
import jax.numpy as jnp
from jax import lax

D = 8192
FL = 14336
RANK = 16
OWN = 3
NBLK = 6
ADAPTERS = 48
TOKENS = 12288
BLOCKS = 96
CAP = 1


def pair_tables(key):
    frozen_base_output = jax.random.fold_in(key, 11)
    key_perm, key_order, key_slot = jax.random.split(frozen_base_output, 3)
    owner_order = jax.random.permutation(key_perm, ADAPTERS)
    replicas = BLOCKS // NBLK
    orders = jax.vmap(lambda sub: jax.random.permutation(sub, replicas))(jax.random.split(key_order, replicas))
    column = jnp.arange(NBLK) // CAP
    target = orders[:, column]
    slot_pick = jax.random.randint(key_slot, (replicas, NBLK), 0, OWN)
    adapter_ids = owner_order[target * OWN + slot_pick]
    return (owner_order.astype(jnp.int32), adapter_ids.reshape(BLOCKS).astype(jnp.int32))


def draw_block_adapter(key, part):
    return pair_tables(key)[1]


def draw_owned_ids(key, part):
    return pair_tables(key)[0]


def block_levels(rng, shape, pieces, least, largest):
    def one(dim, parts):
        heights = jax.random.uniform(jax.random.fold_in(jax.random.fold_in(rng, 6), dim), (parts,), jnp.float32, least / len(pieces), largest / len(pieces))
        return jnp.repeat(jnp.exp(heights), shape[dim] // parts).reshape((-1,) + (1,) * (len(shape) - dim - 1))

    factor_of = one(*pieces[0])
    for cut in pieces[1:]:
        factor_of = factor_of * one(*cut)
    return factor_of


def noise(stream_key, shape, deviation, most, cuts=(), kind=jnp.bfloat16):
    factor_of = block_levels(stream_key, shape, cuts, -0.22, 0.18) if cuts else 1.0
    result = jax.random.normal(stream_key, shape, jnp.float32) * deviation * factor_of
    return jnp.minimum(jnp.maximum(result, -most), most).astype(kind)


def setup_inputs(seed: int = 0) -> dict:
    keys = jax.random.split(jax.random.key(seed), 14)
    return {
        "out_grad": noise(keys[0], (TOKENS, D), 1.0, 6.0, ((0, 16), (1, 16))),
        "block_input": noise(keys[1], (TOKENS, D), 1.0, 6.0, ((0, 16), (1, 16))),
        "gate_pre": noise(keys[2], (TOKENS, FL), 1.5, 8.0, ((0, 16), (1, 16))),
        "up_pre": noise(keys[3], (TOKENS, FL), 1.0, 6.0, ((0, 16), (1, 16))),
        "down_weight": noise(keys[4], (FL, D), FL ** -0.5, 0.046875, ((0, 16), (1, 16))),
        "gate_in": noise(keys[5], (ADAPTERS, RANK, D), D ** -0.5, 0.0625, ((2, 16),)),
        "gate_adapter_output_maps": noise(keys[6], (ADAPTERS, RANK, FL), FL ** -0.5, 0.046875, ((2, 16),)),
        "up_in": noise(keys[7], (ADAPTERS, RANK, D), D ** -0.5, 0.0625, ((2, 16),)),
        "up_adapter_output_maps": noise(keys[8], (ADAPTERS, RANK, FL), FL ** -0.5, 0.046875, ((2, 16),)),
        "down_in": noise(keys[9], (ADAPTERS, RANK, FL), FL ** -0.5, 0.046875, ((2, 16),)),
        "down_out": noise(keys[10], (ADAPTERS, RANK, D), D ** -0.5, 0.0625, ((2, 16),)),
        "block_adapter": draw_block_adapter(jax.random.fold_in(keys[13], 71), 0),
        "owned_ids": draw_owned_ids(jax.random.fold_in(keys[13], 71), 0),
    }


adapter_scale_factor = 2.0


def reference(out_grad, block_input, gate_pre, up_pre, down_weight, gate_in, gate_adapter_output_maps, up_in, up_adapter_output_maps, down_in, down_out, block_adapter, owned_ids):
    block_count = block_adapter.shape[0]
    rows_per_block = out_grad.shape[0] // block_count
    width = out_grad.shape[1]
    hidden_width = gate_pre.shape[1]
    adapters = owned_ids.shape[0]

    def selected_adapter(table):
        return jnp.take(table, block_adapter, axis=0).astype(jnp.float32)

    output_grad_blocks = out_grad.reshape(block_count, rows_per_block, width).astype(jnp.float32)
    input_blocks = block_input.reshape(block_count, rows_per_block, width).astype(jnp.float32)
    gate_f = gate_pre.reshape(block_count, rows_per_block, hidden_width).astype(jnp.float32)
    up_f = up_pre.reshape(block_count, rows_per_block, hidden_width).astype(jnp.float32)
    g_in = selected_adapter(gate_in)
    u_in = selected_adapter(up_in)
    input_dimension = selected_adapter(down_in)
    rank_gate_projection = jnp.einsum('nbd,nrd->nrb', input_blocks, g_in).astype(jnp.bfloat16)
    rank_up_projection = jnp.einsum('nbd,nrd->nrb', input_blocks, u_in).astype(jnp.bfloat16)
    hidden_activation = (jax.nn.silu(gate_f) * up_f).astype(jnp.bfloat16)
    rank_down_projection = jnp.einsum('cil,col->coi', hidden_activation.astype(jnp.float32), input_dimension).astype(jnp.bfloat16)
    down_error_signal = jnp.einsum('nbd,nrd->nrb', output_grad_blocks, selected_adapter(down_out)).astype(jnp.bfloat16)
    frozen_base_output = jnp.dot(out_grad, down_weight.T, preferred_element_type=jnp.float32).reshape(block_count, rows_per_block, hidden_width)
    hidden_gradient_rows = frozen_base_output + adapter_scale_factor * jnp.einsum('elz,elp->ezp', down_error_signal.astype(jnp.float32), input_dimension)
    sigmoid_gate = jax.nn.sigmoid(gate_f)
    gate_gradient_total = (hidden_gradient_rows * up_f * sigmoid_gate * (1.0 + gate_f * (1.0 - sigmoid_gate))).astype(jnp.bfloat16)
    up_gradient_total = (hidden_gradient_rows * gate_f * sigmoid_gate).astype(jnp.bfloat16)
    gate_backward = (adapter_scale_factor * jnp.einsum('cil,col->coi', gate_gradient_total.astype(jnp.float32), selected_adapter(gate_adapter_output_maps))).astype(jnp.bfloat16)
    up_backward = (adapter_scale_factor * jnp.einsum('cil,col->coi', up_gradient_total.astype(jnp.float32), selected_adapter(up_adapter_output_maps))).astype(jnp.bfloat16)
    input_grad = jnp.einsum('nrb,nrd->nbd', gate_backward.astype(jnp.float32), g_in) + jnp.einsum('nrb,nrd->nbd', up_backward.astype(jnp.float32), u_in)
    input_grad = input_grad.astype(jnp.bfloat16).reshape(block_count * rows_per_block, width)

    def outer_product_sum(low, right):
        return jnp.einsum('nrb,nbw->nrw', low.astype(jnp.float32), right.astype(jnp.float32))

    gradient_messages = [outer_product_sum(gate_backward, input_blocks), adapter_scale_factor * outer_product_sum(rank_gate_projection, gate_gradient_total), outer_product_sum(up_backward, input_blocks), adapter_scale_factor * outer_product_sum(rank_up_projection, up_gradient_total), adapter_scale_factor * outer_product_sum(down_error_signal, hidden_activation), adapter_scale_factor * outer_product_sum(rank_down_projection, output_grad_blocks)]
    member = (block_adapter[None, :] == jnp.arange(adapters)[:, None]).astype(jnp.float32)
    results = []
    for packet in gradient_messages:
        summed = jnp.einsum('an,nrw->arw', member, packet, precision=lax.Precision.HIGHEST)
        results.append(jnp.take(summed, owned_ids, axis=0))
    return (input_grad, results[0], results[1], results[2], results[3], results[4], results[5])
```

```python
import heapq

import jax
import jax.numpy as jnp
from jax import lax
from jax.experimental import pallas as pl
from jax.experimental.pallas import tpu as pltpu
from jax.sharding import PartitionSpec as P

SCALE = 2.0
F32 = jnp.float32
BF16 = jnp.bfloat16
MESH = pl.DeviceIdType.MESH
RING = 4
DEPTH = 8


def centred(a):
    return ((a + 1) % RING) - 1


def weight_hops(kind, u, v):
    sign = 1 if kind % 2 == 0 else -1
    first, second = ("x", "y") if kind < 2 else ("y", "x")
    hops = []
    if v == 0:
        if u == 0:
            hops += [(first, sign), (first, -sign)]
        elif u == -sign:
            hops += [(first, sign)]
        hops += [(second, sign), (second, -sign)]
    elif v == -sign:
        hops += [(second, sign)]
    return first, hops


def weight_timeline(unit):
    free = {(a, s): 0.0 for a in "xy" for s in (1, -1)}
    order, count = [], 0
    heap = [(0.0, k - 4, k, 0, 0) for k in range(4)]
    heapq.heapify(heap)
    while heap:
        now, _, kind, u, v = heapq.heappop(heap)
        order.append((now, kind, u, v))
        first, hops = weight_hops(kind, u, v)
        for axis, sign in hops:
            end = max(free[(axis, sign)], now) + unit
            free[(axis, sign)] = end
            nu, nv = (centred(u - sign), v) if axis == first else (u, centred(v - sign))
            heapq.heappush(heap, (end + 1.5, count, kind, nu, nv))
            count += 1
    return order


def rows_dot(a, b):
    return lax.dot_general(a, b, (((1,), (1,)), ((), ())), preferred_element_type=F32)


def turned_dot(a, b):
    return jnp.dot(a.astype(F32).T.astype(BF16), b, preferred_element_type=F32)


def kernel(
    dims,
    dy_h, x_h, gp_h, up_h, w_h, gin_h, gout_h, uin_h, uout_h, din_h, dout_h, ids, owned,
    ig_h, o_gin, o_gout, o_uin, o_uout, o_din, o_dout,
    dyf, wf, xb, gp, up, tw, tf, fa, fb, hid, acc, part1, red1, res1, part2, red2, res2, big, pick,
    s_d, s_o, s_i, r_d, r_o, r_i, ig, st_w, st_f,
    loc_sem, out_sem, dsend, drecv, csend, crecv, wsend, wrecv,
    rs1s, rs1r, ag1s, ag1r, rs2s, rs2r, ag2s, ag2r, a2s, a2r,
):
    NB, RB, WD, FW, NQ, NS, OWN, RK = dims
    q = lax.axis_index("dp")
    s = lax.axis_index("tensor")
    x, y = q // RING, q % RING
    z, c = s // 2, s % 2

    def dp_at(axis, sign):
        if axis == "x":
            return ((x + sign + RING) % RING) * RING + y
        return x * RING + (y + sign + RING) % RING

    def to_dp(qq):
        return {"dp": qq, "tensor": s}

    def to_tensor(ss):
        return {"dp": q, "tensor": ss}

    def z_at(off):
        return (z + off + DEPTH) % DEPTH

    def remote(src, dst, ss, rs, dev):
        return pltpu.make_async_remote_copy(
            src_ref=src, dst_ref=dst, send_sem=ss, recv_sem=rs, device_id=dev, device_id_type=MESH
        )

    loads = [
        (dy_h, dyf.at[s]), (x_h, xb), (gp_h, gp), (up_h, up), (w_h, wf.at[q]),
        (gin_h, tw.at[0]), (uin_h, tw.at[1]), (dout_h, tw.at[2]),
        (gout_h, tf.at[0]), (uout_h, tf.at[1]), (din_h, tf.at[2]),
    ]
    loads = [pltpu.make_async_copy(a, b, loc_sem.at[i]) for i, (a, b) in enumerate(loads)]

    barrier = pltpu.get_barrier_semaphore()
    peers = [to_dp(dp_at(a, sg)) for a in "xy" for sg in (1, -1)]
    peers += [to_tensor(z_at(1) * 2 + c), to_tensor(z_at(-1) * 2 + c), to_tensor(z * 2 + 1 - c)]
    for peer in peers:
        pl.semaphore_signal(barrier, inc=1, device_id=peer, device_id_type=MESH)
    pl.semaphore_wait(barrier, len(peers))

    QR = wf.shape[1] // 4
    wcount = [0]

    def wpiece(kind, u, v):
        ox, oy = (u, v) if kind < 2 else (v, u)
        qq = ((x + ox + RING) % RING) * RING + (y + oy + RING) % RING
        return wf.at[qq, pl.ds(kind * QR, QR), :]

    def wsem(kind, u, v):
        return kind * 16 + (u % RING) * RING + v % RING

    def wforward(kind, u, v):
        first, hops = weight_hops(kind, u, v)
        piece = wpiece(kind, u, v)
        src = w_h.at[pl.ds(kind * QR, QR), :] if (u, v) == (0, 0) else piece
        for axis, sign in hops:
            nu, nv = (centred(u - sign), v) if axis == first else (u, centred(v - sign))
            remote(
                src, piece, wsend.at[wcount[0]], wrecv.at[wsem(kind, nu, nv)], to_dp(dp_at(axis, sign))
            ).start()
            wcount[0] += 1

    def wwait(kind, u, v):
        piece = wpiece(kind, u, v)
        remote(piece, piece, wsend.at[0], wrecv.at[wsem(kind, u, v)], to_dp(q)).wait_recv()

    HR = dyf.shape[1] // 2
    dcount = [0]
    ccount = [0]

    def dpiece(off, h, core):
        return dyf.at[z_at(off) * 2 + core, pl.ds(h * HR, HR), :]

    def dsem(off, h):
        return (off % DEPTH) * 2 + h

    def dforward(off, h):
        piece = dpiece(off, h, c)
        src = dy_h.at[pl.ds(h * HR, HR), :] if off == 0 else piece
        going = []
        if off <= 0 and (off > -3 or (off == -3 and h == 0)):
            going.append(1)
        if off >= 0 and (off < 3 or (off == 3 and h == 1)):
            going.append(-1)
        for sign in going:
            to = off - sign
            remote(
                src, piece, dsend.at[dcount[0]], drecv.at[dsem(to, h)], to_tensor(z_at(sign) * 2 + c)
            ).start()
            dcount[0] += 1
        remote(
            src, piece, csend.at[ccount[0]], crecv.at[dsem(off, h)], to_tensor(z * 2 + 1 - c)
        ).start()
        ccount[0] += 1

    def dwait(off, h):
        piece = dpiece(off, h, c)
        remote(piece, piece, dsend.at[0], drecv.at[dsem(off, h)], to_tensor(s)).wait_recv()

    def cwait(off, h):
        piece = dpiece(off, h, 1 - c)
        remote(piece, piece, csend.at[0], crecv.at[dsem(off, h)], to_tensor(s)).wait_recv()

    for kind in range(4):
        wforward(kind, 0, 0)
    for h in range(2):
        dforward(0, h)
    for cp in loads:
        cp.start()

    ids_me = [ids[q * NB + n] for n in range(NB)]

    def rows(n):
        return pl.ds(n * RB, RB)

    def act(n):
        @pl.loop(0, RB // 16)
        def _(i):
            r = pl.ds(pl.multiple_of(n * RB + i * 16, 16), 16)
            g = gp[r, :].astype(F32)
            u = up[r, :].astype(F32)
            sg = jax.nn.sigmoid(g)
            b = g * sg
            fb[r, :] = b
            fa[r, :] = u * sg * (1.0 + g * (1.0 - sg))
            hid[r, :] = (b * u).astype(BF16)

    def ranks(n):
        a = ids_me[n]
        part1[n] = rows_dot(tw[0, a], xb[rows(n), :])
        part1[NB + n] = rows_dot(tw[1, a], xb[rows(n), :])
        part1[2 * NB + n] = rows_dot(tf[2, a], hid[rows(n), :])
        part1[3 * NB + n] = rows_dot(tw[2, a], dyf[s, rows(n), :])

    def picker():
        row = lax.broadcasted_iota(jnp.int32, (OWN * RK, NQ * RK), 0)
        col = lax.broadcasted_iota(jnp.int32, (OWN * RK, NQ * RK), 1)
        same = (row % RK) == (col % RK)
        rown, cown = row // RK, col // RK

        def body(qq, m):
            for o in range(OWN):
                mine = owned[q * OWN + o]
                hit = jnp.int32(0)
                for n in range(NB):
                    hit = hit + jnp.where(ids[qq * NB + n] == mine, 1, 0)
                val = jnp.where(hit > 0, 1.0, 0.0).astype(F32)
                m = m + jnp.where((cown == qq) & (rown == o) & same, 1.0, 0.0) * val
            return m

        pick[...] = lax.fori_loop(0, NQ, body, jnp.zeros((OWN * RK, NQ * RK), F32)).astype(BF16)

    def waits(a, b):
        def run():
            for cp in loads[a:b]:
                cp.wait()

        return run

    acc_rows = 256

    def product(ox, oy, fresh=False):
        k = ((x + ox + RING) % RING) * RING + (y + oy + RING) % RING

        @pl.loop(0, acc.shape[0] // acc_rows)
        def _(m):
            r = pl.ds(pl.multiple_of(m * acc_rows, acc_rows), acc_rows)
            d = rows_dot(dyf[k, r, :], wf[k])
            acc[r, :] = d if fresh else acc[r, :] + d

    def scatter(part, red, count, ssem, rsem):
        def one(t, _):
            to = (s + t) % NS
            for lane in range((count + NS - 1) // NS):
                def send(lane=lane, to=to):
                    remote(
                        part.at[lane * NS + to], red.at[lane, s], ssem.at[lane, t], rsem.at[lane, s], to_tensor(to)
                    ).start()
                if (lane + 1) * NS <= count:
                    send()
                else:
                    pl.when(to < count - lane * NS)(send)
            return 0

        lax.fori_loop(1, NS, one, 0)

    def gather_sum(part, red, res, count, rsem, ssem2, rsem2):
        for lane in range((count + NS - 1) // NS):
            def go(lane=lane):
                def wait(t, _):
                    src = (s + NS - t) % NS
                    remote(
                        red.at[lane, src], red.at[lane, src], ssem2.at[0, 0], rsem.at[lane, src], to_tensor(s)
                    ).wait_recv()
                    return 0

                lax.fori_loop(1, NS, wait, 0)
                red[lane, s] = part[lane * NS + s]
                total = red[lane, 0]
                for t in range(1, NS):
                    total = total + red[lane, t]
                res[lane * NS + s] = total.astype(BF16)

                def send(t, _):
                    to = (s + t) % NS
                    piece = res.at[lane * NS + s]
                    remote(piece, piece, ssem2.at[lane, t], rsem2.at[lane, s], to_tensor(to)).start()
                    return 0

                lax.fori_loop(1, NS, send, 0)
            if (lane + 1) * NS <= count:
                go()
            else:
                pl.when(s < count - lane * NS)(go)

    def gather_wait(res, count, ssem2, rsem2):
        def one(t, _):
            src = (s + NS - t) % NS
            for lane in range((count + NS - 1) // NS):
                def wait(lane=lane, src=src):
                    piece = res.at[lane * NS + src]
                    remote(piece, piece, ssem2.at[0, 0], rsem2.at[lane, src], to_tensor(s)).wait_recv()
                if (lane + 1) * NS <= count:
                    wait()
                else:
                    pl.when(src < count - lane * NS)(wait)
            return 0

        lax.fori_loop(1, NS, one, 0)

    def sent(part, res, count, ssem, ssem2):
        def one(t, _):
            to = (s + t) % NS
            for lane in range((count + NS - 1) // NS):
                def wait1(lane=lane, to=to):
                    piece = part.at[lane * NS + to]
                    remote(piece, piece, ssem.at[lane, t], ssem.at[lane, t], to_tensor(s)).wait_send()

                def wait2(lane=lane):
                    piece = res.at[lane * NS + s]
                    remote(piece, piece, ssem2.at[lane, t], ssem2.at[lane, t], to_tensor(s)).wait_send()
                if (lane + 1) * NS <= count:
                    wait1()
                    wait2()
                else:
                    pl.when(to < count - lane * NS)(wait1)
                    pl.when(s < count - lane * NS)(wait2)
            return 0

        lax.fori_loop(1, NS, one, 0)

    def spread(res, base):
        def body(qq, _):
            for n in range(NB):
                hit = jnp.int32(0)
                for o in range(OWN):
                    hit = hit + jnp.where(owned[qq * OWN + o] == ids_me[n], 1, 0)
                val = jnp.where(hit > 0, 1.0, 0.0).astype(F32)
                big[pl.ds(pl.multiple_of(qq * RK, RK), RK), n * RB : (n + 1) * RB] = (
                    res[base + n].astype(F32) * val
                ).astype(BF16)
            return 0

        lax.fori_loop(0, NQ, body, 0)

    def packet(res, base, right, out, lo, hi, scale):
        spread(res, base)
        d = jnp.dot(big[...], right, preferred_element_type=F32)
        if scale != 1.0:
            d = d * scale
        out[:, :, lo:hi] = d.astype(BF16).reshape(NQ, RK, hi - lo)

    def exchange(g, src, dst):
        def one(t, _):
            to = (q + t) % NQ
            remote(src.at[to], dst.at[q], a2s.at[g, t], a2r.at[g, q], to_dp(to)).start()
            return 0

        lax.fori_loop(1, NQ, one, 0)
        dst[q] = src[q]

    def exchanged(g, dst):
        def one(t, _):
            src = (q + NQ - t) % NQ
            remote(dst.at[src], dst.at[src], a2s.at[g, 0], a2r.at[g, src], to_dp(q)).wait_recv()
            return 0

        lax.fori_loop(1, NQ, one, 0)

    def exchange_sent(g, src):
        def one(t, _):
            to = (q + t) % NQ
            remote(src.at[to], src.at[to], a2s.at[g, t], a2r.at[g, 0], to_dp(q)).wait_send()
            return 0

        lax.fori_loop(1, NQ, one, 0)

    outs = []

    def put(src, dst):
        cp = pltpu.make_async_copy(src, dst, out_sem.at[len(outs)])
        cp.start()
        outs.append(cp)

    def collect(dst, lo, hi, stage, out):
        d = jnp.dot(pick[...], dst[:, :, lo:hi].reshape(NQ * RK, hi - lo), preferred_element_type=F32)
        stage[...] = d.reshape(OWN, RK, hi - lo)
        put(stage, out)

    unit = 4.93
    events = []
    for now, kind, u, v in weight_timeline(unit):
        if (u, v) != (0, 0):
            events.append((now, "w", (kind, u, v)))
    for d in range(1, 5):
        for h in range(2):
            for off in (-d, d):
                if d == 4 and (off < 0) != (h == 0):
                    continue
                when = 1.5 + unit * 12 / 7 * (2 * (d - 1) + (h if d < 4 else 0) + 1)
                events.append((when, "d", (off, h)))
    last_dy = max(e[0] for e in events if e[1] == "d")
    ready = {}
    for now, what, a in events:
        if what == "w":
            o = (a[1], a[2]) if a[0] < 2 else (a[2], a[1])
            ready[o] = max(ready.get(o, 0.0), now)
    ready[(0, 0)] = 0.0
    pieces = [(2.0, waits(2, 4))] + [(2.5 + 1.0 * n, lambda n=n: act(n)) for n in range(NB)]
    pieces += [(9.0, waits(0, 2)), (9.0, waits(4, 11))]
    pieces += [(12.0 + 4.0 * n, lambda n=n: ranks(n)) for n in range(NB)]
    pieces += [(40.0, picker)]

    def dy_done():
        for off in list(range(-3, 5)):
            for h in range(2):
                cwait(off, h)
        scatter(part1, red1, 4 * NB, rs1s, rs1r)

    pieces += [(last_dy + 1.5, dy_done)]
    at = last_dy + 1.6
    for i, (o, when) in enumerate(sorted(ready.items(), key=lambda kv: (kv[1], kv[0]))):
        at = max(at + 1.2, when + 0.1)
        pieces.append((at, lambda o=o, i=i: product(o[0], o[1], i == 0)))

    def reduce1():
        gather_sum(part1, red1, res1, 4 * NB, rs1r, ag1s, ag1r)

    def down_packets():
        gather_wait(res1, 4 * NB, ag1s, ag1r)
        packet(res1, 3 * NB, hid[...], s_d, 0, FW, SCALE)
        packet(res1, 2 * NB, dyf[s], s_d, FW, FW + WD, SCALE)
        exchange(0, s_d, r_d)
        for n in range(NB):
            acc[rows(n), :] = acc[rows(n), :] + SCALE * turned_dot(res1[3 * NB + n], tf[2, ids_me[n]])

    pieces += [(last_dy + 7.0, reduce1), (last_dy + 12.0, down_packets)]

    line = [(e[0], i, e[1], e[2]) for i, e in enumerate(events)]
    line += [(t, 1000 + i, "c", f) for i, (t, f) in enumerate(pieces)]
    for _, _, what, a in sorted(line, key=lambda e: (e[0], e[1])):
        if what == "w":
            wwait(*a)
            wforward(*a)
        elif what == "d":
            dwait(*a)
            dforward(*a)
        else:
            a()

    @pl.loop(0, acc.shape[0] // 16)
    def _(i):
        r = pl.ds(pl.multiple_of(i * 16, 16), 16)
        h = acc[r, :]
        gp[r, :] = (h * fa[r, :]).astype(BF16)
        up[r, :] = (h * fb[r, :]).astype(BF16)

    for n in range(NB):
        part2[n] = SCALE * rows_dot(tf[0, ids_me[n]], gp[rows(n), :])
        part2[NB + n] = SCALE * rows_dot(tf[1, ids_me[n]], up[rows(n), :])
    scatter(part2, red2, 2 * NB, rs2s, rs2r)
    packet(res1, 0, gp[...], s_o, 0, FW, SCALE)
    packet(res1, NB, up[...], s_o, FW, 2 * FW, SCALE)
    exchange(1, s_o, r_o)
    gather_sum(part2, red2, res2, 2 * NB, rs2r, ag2s, ag2r)
    exchanged(0, r_d)
    collect(r_d, 0, FW, st_f.at[0], o_din)
    collect(r_d, FW, FW + WD, st_w.at[0], o_dout)
    gather_wait(res2, 2 * NB, ag2s, ag2r)
    packet(res2, 0, xb[...], s_i, 0, WD, 1.0)
    packet(res2, NB, xb[...], s_i, WD, 2 * WD, 1.0)
    exchange(2, s_i, r_i)
    for n in range(NB):
        a = ids_me[n]
        d = turned_dot(res2[n], tw[0, a]) + turned_dot(res2[NB + n], tw[1, a])
        ig[rows(n), :] = d.astype(BF16)
    put(ig, ig_h)
    exchanged(1, r_o)
    collect(r_o, 0, FW, st_f.at[1], o_gout)
    collect(r_o, FW, 2 * FW, st_f.at[2], o_uout)
    exchanged(2, r_i)
    collect(r_i, 0, WD, st_w.at[1], o_gin)
    collect(r_i, WD, 2 * WD, st_w.at[2], o_uin)

    for i in range(wcount[0]):
        piece = wf.at[0, pl.ds(0, QR), :]
        remote(piece, piece, wsend.at[i], wrecv.at[0], to_dp(q)).wait_send()
    for i in range(dcount[0]):
        piece = dyf.at[0, pl.ds(0, HR), :]
        remote(piece, piece, dsend.at[i], drecv.at[0], to_tensor(s)).wait_send()
    for i in range(ccount[0]):
        piece = dyf.at[0, pl.ds(0, HR), :]
        remote(piece, piece, csend.at[i], crecv.at[0], to_tensor(s)).wait_send()
    sent(part1, res1, 4 * NB, rs1s, ag1s)
    sent(part2, res2, 2 * NB, rs2s, ag2s)
    exchange_sent(0, s_d)
    exchange_sent(1, s_o)
    exchange_sent(2, s_i)
    for cp in outs:
        cp.wait()


def shards(dy, xin, gpre, upre, w, gin, gout, uin, uout, din, dout, ids, owned):
    NQ, NS = lax.axis_size("dp"), lax.axis_size("tensor")
    T, WD = dy.shape
    FW = gpre.shape[1]
    A, RK = gin.shape[:2]
    NB = ids.shape[0] // NQ
    OWN = A // NQ
    RB = T // NB
    dims = (NB, RB, WD, FW, NQ, NS, OWN, RK)
    any_ = pl.BlockSpec(memory_space=pl.ANY)
    smem = pl.BlockSpec(memory_space=pltpu.SMEM)
    V = pltpu.VMEM
    D = pltpu.SemaphoreType.DMA
    outs = (
        jax.ShapeDtypeStruct((T, WD), BF16),
        jax.ShapeDtypeStruct((OWN, RK, WD), F32),
        jax.ShapeDtypeStruct((OWN, RK, FW), F32),
        jax.ShapeDtypeStruct((OWN, RK, WD), F32),
        jax.ShapeDtypeStruct((OWN, RK, FW), F32),
        jax.ShapeDtypeStruct((OWN, RK, FW), F32),
        jax.ShapeDtypeStruct((OWN, RK, WD), F32),
    )
    scratch = [
        V((NS, T, WD), BF16), V((NQ,) + w.shape, BF16), V((T, WD), BF16), V((T, FW), BF16), V((T, FW), BF16),
        V((3, A, RK, WD), BF16), V((3, A, RK, FW), BF16),
        V((T, FW), F32), V((T, FW), F32), V((T, FW), BF16), V((T, FW), F32),
        V((4 * NB, RK, RB), F32), V((2, NS, RK, RB), F32), V((4 * NB, RK, RB), BF16),
        V((2 * NB, RK, RB), F32), V((1, NS, RK, RB), F32), V((2 * NB, RK, RB), BF16),
        V((NQ * RK, T), BF16), V((OWN * RK, NQ * RK), BF16),
        V((NQ, RK, FW + WD), BF16), V((NQ, RK, 2 * FW), BF16), V((NQ, RK, 2 * WD), BF16),
        V((NQ, RK, FW + WD), BF16), V((NQ, RK, 2 * FW), BF16), V((NQ, RK, 2 * WD), BF16),
        V((T, WD), BF16), V((3, OWN, RK, WD), F32), V((3, OWN, RK, FW), F32),
        D((11,)), D((7,)), D((14,)), D((16,)), D((16,)), D((16,)), D((60,)), D((64,)),
        D((2, NS)), D((2, NS)), D((2, NS)), D((2, NS)), D((1, NS)), D((1, NS)), D((1, NS)), D((1, NS)),
        D((3, NQ)), D((3, NQ)),
    ]
    return pl.pallas_call(
        lambda *refs: kernel(dims, *refs),
        out_shape=outs,
        in_specs=[any_] * 11 + [smem] * 2,
        out_specs=tuple([any_] * 7),
        scratch_shapes=scratch,
        compiler_params=pltpu.CompilerParams(
            collective_id=0, has_side_effects=True, vmem_limit_bytes=67043328
        ),
        name="step",
    )(dy, xin, gpre, upre, w, gin, gout, uin, uout, din, dout, ids, owned)


def solution(mesh):
    wide = P("dp", "tensor")
    table = P(None, None, "tensor")
    owner = P("dp", None, "tensor")
    return jax.shard_map(
        shards,
        mesh=mesh,
        in_specs=(wide,) * 4 + (P("tensor", "dp"),) + (table,) * 6 + (P(), P()),
        out_specs=(wide,) + (owner,) * 6,
        check_vma=False,
    )
```

```python
import heapq

import jax
import jax.numpy as jnp
from jax import lax
from jax.experimental import pallas as pl
from jax.experimental.pallas import tpu as pltpu
from jax.sharding import PartitionSpec as P

SCALE = 2.0
F32 = jnp.float32
BF16 = jnp.bfloat16
MESH = pl.DeviceIdType.MESH
RING = 4
DEPTH = 8


def centred(a):
    return ((a + 1) % RING) - 1


def weight_hops(kind, u, v):
    sign = 1 if kind % 2 == 0 else -1
    first, second = ("x", "y") if kind < 2 else ("y", "x")
    hops = []
    if v == 0:
        if u == 0:
            hops += [(first, sign), (first, -sign)]
        elif u == -sign:
            hops += [(first, sign)]
        hops += [(second, sign), (second, -sign)]
    elif v == -sign:
        hops += [(second, sign)]
    return first, hops


def weight_timeline(unit):
    free = {(a, s): 0.0 for a in "xy" for s in (1, -1)}
    order, count = [], 0
    heap = [(0.0, k - 4, k, 0, 0) for k in range(4)]
    heapq.heapify(heap)
    while heap:
        now, _, kind, u, v = heapq.heappop(heap)
        order.append((now, kind, u, v))
        first, hops = weight_hops(kind, u, v)
        for axis, sign in hops:
            end = max(free[(axis, sign)], now) + unit
            free[(axis, sign)] = end
            nu, nv = (centred(u - sign), v) if axis == first else (u, centred(v - sign))
            heapq.heappush(heap, (end + 1.5, count, kind, nu, nv))
            count += 1
    return order


def rows_dot(a, b):
    return lax.dot_general(a, b, (((1,), (1,)), ((), ())), preferred_element_type=F32)


def turned_dot(a, b):
    return jnp.dot(a.astype(F32).T.astype(BF16), b, preferred_element_type=F32)


def kernel(
    dims,
    dy_h, x_h, gp_h, up_h, w_h, gin_h, gout_h, uin_h, uout_h, din_h, dout_h, ids, owned,
    ig_h, o_gout, o_uout, o_din, o_dout, r_i, pick_h,
    dyf, wf, xb, gp, up, tw, tf, fa, fb, hid, acc, part1, red1, res1, part2, red2, res2, big, mask, pick,
    s_d, s_o, s_i, r_d, r_o, ig, st_w, st_f,
    loc_sem, out_sem, dsend, drecv, csend, crecv, wsend, wrecv,
    rs1s, rs1r, ag1s, ag1r, rs2s, rs2r, ag2s, ag2r, a2s, a2r,
):
    NB, RB, WD, FW, NQ, NS, OWN, RK = dims
    q = lax.axis_index("dp")
    s = lax.axis_index("tensor")
    x, y = q // RING, q % RING
    z, c = s // 2, s % 2

    def dp_at(axis, sign):
        if axis == "x":
            return ((x + sign + RING) % RING) * RING + y
        return x * RING + (y + sign + RING) % RING

    def to_dp(qq):
        return {"dp": qq, "tensor": s}

    def to_tensor(ss):
        return {"dp": q, "tensor": ss}

    def z_at(off):
        return (z + off + DEPTH) % DEPTH

    def remote(src, dst, ss, rs, dev):
        return pltpu.make_async_remote_copy(
            src_ref=src, dst_ref=dst, send_sem=ss, recv_sem=rs, device_id=dev, device_id_type=MESH
        )

    loads = [
        (gp_h, gp), (up_h, up), (dy_h, dyf.at[s]), (x_h, xb), (w_h, wf.at[q]),
        (gin_h, tw.at[0]), (uin_h, tw.at[1]), (dout_h, tw.at[2]),
        (gout_h, tf.at[0]), (uout_h, tf.at[1]), (din_h, tf.at[2]),
    ]
    loads = [pltpu.make_async_copy(a, b, loc_sem.at[i]) for i, (a, b) in enumerate(loads)]

    barrier = pltpu.get_barrier_semaphore()
    peers = [to_dp(dp_at(a, sg)) for a in "xy" for sg in (1, -1)]
    peers += [to_tensor(z_at(1) * 2 + c), to_tensor(z_at(-1) * 2 + c), to_tensor(z * 2 + 1 - c)]
    for peer in peers:
        pl.semaphore_signal(barrier, inc=1, device_id=peer, device_id_type=MESH)
    pl.semaphore_wait(barrier, len(peers))

    QR = wf.shape[1] // 4
    wcount = [0]

    def wpiece(kind, u, v):
        ox, oy = (u, v) if kind < 2 else (v, u)
        qq = ((x + ox + RING) % RING) * RING + (y + oy + RING) % RING
        return wf.at[qq, pl.ds(kind * QR, QR), :]

    def wsem(kind, u, v):
        return kind * 16 + (u % RING) * RING + v % RING

    def wforward(kind, u, v):
        first, hops = weight_hops(kind, u, v)
        piece = wpiece(kind, u, v)
        src = w_h.at[pl.ds(kind * QR, QR), :] if (u, v) == (0, 0) else piece
        for axis, sign in hops:
            nu, nv = (centred(u - sign), v) if axis == first else (u, centred(v - sign))
            remote(
                src, piece, wsend, wrecv.at[wsem(kind, nu, nv)], to_dp(dp_at(axis, sign))
            ).start()
            wcount[0] += 1

    def wwait(kind, u, v):
        piece = wpiece(kind, u, v)
        remote(piece, piece, wsend, wrecv.at[wsem(kind, u, v)], to_dp(q)).wait_recv()

    HR = dyf.shape[1] // 4
    dcount = [0]
    ccount = [0]

    def dpiece(off, j, core):
        return dyf.at[z_at(off) * 2 + core, pl.ds(j * HR, HR), :]

    def dsem(off, j):
        return (off % DEPTH) * 4 + j

    def dsend_one(off, j, sign):
        piece = dpiece(off, j, c)
        src = dy_h.at[pl.ds(j * HR, HR), :] if off == 0 else piece
        remote(
            src, piece, dsend, drecv.at[dsem(off - sign, j)], to_tensor(z_at(sign) * 2 + c)
        ).start()
        dcount[0] += 1

    def dshare(off, j):
        piece = dpiece(off, j, c)
        src = dy_h.at[pl.ds(j * HR, HR), :] if off == 0 else piece
        remote(
            src, piece, csend, crecv.at[j // 2], to_tensor(z * 2 + 1 - c)
        ).start()
        ccount[0] += 1

    lane = [(0, 0), (0, 1), (0, 2), (1, 0), (1, 1), (0, 3), (2, 0), (2, 1), (1, 2), (3, 0), (1, 3), (2, 2), (2, 3), (3, 2)]
    waiting = {sign: [(-sign * d, j if sign > 0 else j ^ 1) for d, j in lane] for sign in (1, -1)}
    held = {(0, j) for j in range(4)}

    def dflush():
        for sign in (1, -1):
            while waiting[sign] and waiting[sign][0] in held:
                dsend_one(*waiting[sign].pop(0), sign)

    def dforward(off, j):
        held.add((off, j))
        dflush()
        dshare(off, j)

    def dwait(off, j):
        piece = dpiece(off, j, c)
        remote(piece, piece, dsend, drecv.at[dsem(off, j)], to_tensor(s)).wait_recv()

    def cwait():
        both = dyf.at[pl.ds(0, DEPTH // 2)]
        return lambda p: remote(both, both, csend, crecv.at[p], to_tensor(s)).wait_recv()

    for kind in range(4):
        wforward(kind, 0, 0)
    dflush()
    for j in range(4):
        dshare(0, j)
    for cp in loads:
        cp.start()

    outs = []

    def put(src, dst):
        cp = pltpu.make_async_copy(src, dst, out_sem.at[len(outs)])
        cp.start()
        outs.append(cp)

    ids_me = [ids[q * NB + n] for n in range(NB)]

    def rows(n):
        return pl.ds(n * RB, RB)

    def act(n):
        @pl.loop(0, RB // 16)
        def _(i):
            r = pl.ds(pl.multiple_of(n * RB + i * 16, 16), 16)
            g = gp[r, :].astype(F32)
            u = up[r, :].astype(F32)
            sg = jax.nn.sigmoid(g)
            b = g * sg
            fb[r, :] = b
            fa[r, :] = u * sg * (1.0 + g * (1.0 - sg))
            hid[r, :] = (b * u).astype(BF16)

    def ranks(n):
        a = ids_me[n]
        slab(part1, n)[...] = rows_dot(tw[0, a], xb[rows(n), :])
        slab(part1, NB + n)[...] = rows_dot(tw[1, a], xb[rows(n), :])
        slab(part1, 2 * NB + n)[...] = rows_dot(tf[2, a], hid[rows(n), :])
        slab(part1, 3 * NB + n)[...] = rows_dot(tw[2, a], dyf[s, rows(n), :])

    def picker():
        row = lax.broadcasted_iota(jnp.int32, (OWN * RK, NQ * RK), 0)
        col = lax.broadcasted_iota(jnp.int32, (OWN * RK, NQ * RK), 1)
        same = (row % RK) == (col % RK)
        rown, cown = row // RK, col // RK

        def body(qq, m):
            for o in range(OWN):
                mine = owned[q * OWN + o]
                hit = jnp.int32(0)
                for n in range(NB):
                    hit = hit + jnp.where(ids[qq * NB + n] == mine, 1, 0)
                val = jnp.where(hit > 0, 1.0, 0.0).astype(F32)
                m = m + jnp.where((cown == qq) & (rown == o) & same, 1.0, 0.0) * val
            return m

        pick[...] = lax.fori_loop(0, NQ, body, jnp.zeros((OWN * RK, NQ * RK), F32)).astype(BF16)
        put(pick, pick_h)

    def waits(a, b):
        def run():
            for cp in loads[a:b]:
                cp.wait()

        return run

    half_rows = acc.shape[0] // 2

    def product(ox, oy, half, fresh=False):
        if isinstance(oy, tuple):
            oy = oy[0] + (y + oy[0] + c + oy[2]) % 2 * oy[1]
        k = ((x + ox + RING) % RING) * RING + (y + oy + RING) % RING
        r = slice(half * half_rows, (half + 1) * half_rows)
        d = rows_dot(dyf[k, r, :], wf[k])
        acc[r, :] = d if fresh else acc[r, :] + d

    def scatter(part, red, ssem, rsem):
        def one(t, _):
            to = (s + t) % NS

            @pl.when(to < part.shape[0])
            def _():
                remote(part.at[to], red.at[s], ssem, rsem, to_tensor(to)).start()

            return 0

        lax.fori_loop(1, NS, one, 0)

    def gather_sum(part, red, res, rsem, ssem2, rsem2):
        @pl.when(s < part.shape[0])
        def _():
            others_ = red.at[pl.ds(0, NS - 1)]
            remote(others_, others_, ssem2.at[0], rsem, to_tensor(s)).wait_recv()
            red[s] = part[s]
            total = red[0]
            for t in range(1, NS):
                total = total + red[t]
            res[s] = total.astype(BF16)

            def send(t, _):
                to = (s + t) % NS
                remote(res.at[s], res.at[s], ssem2.at[t], rsem2, to_tensor(to)).start()
                return 0

            lax.fori_loop(1, NS, send, 0)

    def each_way(ref, go):
        many = ref.shape[0]
        pl.when(s < many)(lambda: go(ref.at[pl.ds(0, many - 1)]))
        pl.when(s >= many)(lambda: go(ref))

    def gather_wait(res, ssem2, rsem2):
        each_way(res, lambda r: remote(r, r, ssem2.at[0], rsem2, to_tensor(s)).wait_recv())

    def sent(part, res, ssem, ssem2):
        each_way(part, lambda r: remote(r, r, ssem, ssem, to_tensor(s)).wait_send())

        @pl.when(s < res.shape[0])
        def _():
            def one(t, _):
                remote(res.at[s], res.at[s], ssem2.at[t], ssem2.at[t], to_tensor(s)).wait_send()
                return 0

            lax.fori_loop(1, NS, one, 0)

    def slab(ref, i):
        per = ref.shape[1] // RK
        return ref.at[i // per, pl.ds(i % per * RK, RK), :]

    def masks():
        def body(qq, _):
            for n in range(NB):
                hit = jnp.int32(0)
                for o in range(OWN):
                    hit = hit + jnp.where(owned[qq * OWN + o] == ids_me[n], 1, 0)
                val = jnp.where(hit > 0, 1.0, 0.0).astype(F32)
                mask[pl.ds(pl.multiple_of(qq * RK, RK), RK), n * RB : (n + 1) * RB] = jnp.full((RK, RB), val).astype(BF16)
            return 0

        lax.fori_loop(0, NQ, body, 0)

    def spread(res, base):
        row = jnp.concatenate([slab(res, base + n)[...] for n in range(NB)], axis=1)
        for qq in range(NQ):
            big[qq * RK : (qq + 1) * RK, :] = row * mask[qq * RK : (qq + 1) * RK, :]

    def packet(res, base, right, out, lo, hi, scale):
        spread(res, base)
        d = jnp.dot(big[...], right, preferred_element_type=F32)
        if scale != 1.0:
            d = d * scale
        out[:, :, lo:hi] = d.astype(BF16).reshape(NQ, RK, hi - lo)

    ring = (2, 1, -1, 0)
    others = [(a, b) for a in ring for b in ring if (a, b) != (0, 0)]
    others.sort(key=lambda o: -(abs(o[0]) + abs(o[1])))

    def peer(o, sign=1):
        return ((x + sign * o[0] + RING) % RING) * RING + (y + sign * o[1] + RING) % RING

    def exchange(g, src, dst):
        for o in others:
            to = peer(o)
            remote(src.at[to], dst.at[q], a2s.at[g], a2r.at[g], to_dp(to)).start()

    def exchanged(g, dst):
        all_ = dst.at[pl.ds(0, NQ - 1)]
        remote(all_, all_, a2s.at[g], a2r.at[g], to_dp(q)).wait_recv()

    def exchange_sent(g, src):
        all_ = src.at[pl.ds(0, NQ - 1)]
        remote(all_, all_, a2s.at[g], a2r.at[g], to_dp(q)).wait_send()

    def collect(dst, lo, hi, stage, out):
        d = jnp.dot(pick[...], dst[:, :, lo:hi].reshape(NQ * RK, hi - lo), preferred_element_type=F32)
        stage[...] = d.reshape(OWN, RK, hi - lo)
        put(stage, out)

    unit = 4.93
    events = []
    for now, kind, u, v in weight_timeline(unit):
        if (u, v) != (0, 0):
            events.append((now, "w", (kind, u, v)))
    quarter = unit * 12 / 14
    for i, (d, j) in enumerate(lane):
        for sign in (1, -1):
            events.append((3.5 + quarter * (i + 1) + (3.0 if i >= 11 else 0.0), "d", (-sign * (d + 1), j if sign > 0 else j ^ 1)))
    passed = [max(e[0] for e in events if e[1] == "d" and e[2][1] // 2 == p) for p in range(2)]
    ready = {}
    for now, what, a in events:
        if what == "w":
            o = (a[1], a[2]) if a[0] < 2 else (a[2], a[1])
            ready[o] = max(ready.get(o, 0.0), now)
    last_hop = max(e[0] for e in events if e[1] == "w" and len(weight_hops(*e[2])[1]) > 0)
    ready[(0, 0)] = 0.0

    pass_done = cwait()

    def start_ranks():
        scatter(part1, red1, rs1s, rs1r)

    def reduce1():
        gather_sum(part1, red1, res1, rs1r, ag1s, ag1r)

    def down_packets():
        gather_wait(res1, ag1s, ag1r)
        packet(res1, 3 * NB, hid[...], s_d, 0, FW, SCALE)
        packet(res1, 2 * NB, dyf[s], s_d, FW, FW + WD, SCALE)
        r_d[q] = s_d[q]

    def down_out():
        exchange(0, s_d, r_d)

    def adapter_term(n):
        acc[rows(n), :] = acc[rows(n), :] + SCALE * turned_dot(slab(res1, 3 * NB + n)[...], tf[2, ids_me[n]])

    pieces = [(2.0, waits(0, 2))] + [(2.5 + 1.0 * n, lambda n=n: act(n)) for n in range(NB)]
    pieces += [(9.0, waits(2, 11))]
    pieces += [(11.0 + 3.0 * n, lambda n=n: ranks(n)) for n in range(NB)]
    pieces += [(29.5, picker), (32.0, masks)]
    begun = (passed[0] + 5.0, passed[1] + 3.0)
    pieces += [(begun[p], lambda p=p: pass_done(p)) for p in range(2)]
    pieces += [(begun[0] + 0.1, start_ranks), (passed[1] + 0.1, reduce1)]
    pieces += [(last_hop + 1.4, down_packets), (last_hop + 1.5, down_out)]
    by_time = [o for o, _ in sorted(ready.items(), key=lambda kv: (kv[1], kv[0]))]
    first = [(ox, (0, 1, 0)) for ox in (0, -1, 1, 2)] + [(0, (2, -3, 0))]
    second = [(ox, (0, 1, 1)) for ox in (0, -1, 1, 2)] + [(0, (2, -3, 1))]
    paired = [(ox, oy) for ox in (0, -1, 1, 2) for oy in (0, 1)] + [(0, 2), (0, -1)]
    orders = [by_time, first + second + [o for o in by_time if o not in paired]]
    for half in range(2):
        at = (begun[0], passed[1])[half] + 0.2
        for i, o in enumerate(orders[half]):
            at = max(at + 0.5, ready.get(o, 0.0) + 0.1)
            if half == 1 and i == len(first):
                at = max(at, begun[1] + 0.1)
            pieces.append((at, lambda o=o, i=i, half=half: product(o[0], o[1], half, i == 0)))
    pieces += [(last_hop + 1.6 + 0.1 * n, lambda n=n: adapter_term(n)) for n in range(NB)]

    line = [(e[0], i, e[1], e[2]) for i, e in enumerate(events)]
    line += [(t, 1000 + i, "c", f) for i, (t, f) in enumerate(pieces)]
    for _, _, what, a in sorted(line, key=lambda e: (e[0], e[1])):
        if what == "w":
            wwait(*a)
            wforward(*a)
        elif what == "d":
            dwait(*a)
            dforward(*a)
        else:
            a()

    @pl.loop(0, acc.shape[0] // 16)
    def _(i):
        r = pl.ds(pl.multiple_of(i * 16, 16), 16)
        h = acc[r, :]
        gp[r, :] = (h * fa[r, :]).astype(BF16)
        up[r, :] = (h * fb[r, :]).astype(BF16)

    for n in range(NB):
        part2[n] = SCALE * rows_dot(tf[0, ids_me[n]], gp[rows(n), :])
        part2[NB + n] = SCALE * rows_dot(tf[1, ids_me[n]], up[rows(n), :])
    scatter(part2, red2, rs2s, rs2r)
    packet(res1, 0, gp[...], s_o, 0, FW, SCALE)
    packet(res1, NB, up[...], s_o, FW, 2 * FW, SCALE)
    exchange(1, s_o, r_o)
    r_o[q] = s_o[q]
    gather_sum(part2, red2, res2, rs2r, ag2s, ag2r)
    exchanged(0, r_d)
    collect(r_d, 0, FW, st_f.at[0], o_din)
    collect(r_d, FW, FW + WD, st_w, o_dout)
    gather_wait(res2, ag2s, ag2r)
    packet(res2, 0, xb[...], s_i, 0, WD, 1.0)
    packet(res2, NB, xb[...], s_i, WD, 2 * WD, 1.0)
    exchange(2, s_i, r_i)
    put(s_i.at[q], r_i.at[q])
    for n in range(NB):
        a = ids_me[n]
        d = turned_dot(res2[n], tw[0, a]) + turned_dot(res2[NB + n], tw[1, a])
        ig[rows(n), :] = d.astype(BF16)
    put(ig, ig_h)
    exchanged(1, r_o)
    collect(r_o, 0, FW, st_f.at[1], o_gout)
    collect(r_o, FW, 2 * FW, st_f.at[2], o_uout)
    exchanged(2, r_i)

    assert wcount[0] % 4 == dcount[0] % 4 == ccount[0] % 4 == 0
    for ref, many, ss, rs in ((wf, wcount, wsend, wrecv.at[0]), (dyf, dcount, dsend, drecv.at[0]), (dyf, ccount, csend, crecv.at[0])):
        whole = ref.at[pl.ds(0, many[0] // 4)]
        remote(whole, whole, ss, rs, to_dp(q)).wait_send()
    sent(part1, res1, rs1s, ag1s)
    sent(part2, res2, rs2s, ag2s)
    exchange_sent(0, s_d)
    exchange_sent(1, s_o)
    exchange_sent(2, s_i)
    for cp in outs:
        cp.wait()


def shards(dy, xin, gpre, upre, w, gin, gout, uin, uout, din, dout, ids, owned):
    NQ, NS = lax.axis_size("dp"), lax.axis_size("tensor")
    T, WD = dy.shape
    FW = gpre.shape[1]
    A, RK = gin.shape[:2]
    NB = ids.shape[0] // NQ
    OWN = A // NQ
    RB = T // NB
    dims = (NB, RB, WD, FW, NQ, NS, OWN, RK)
    any_ = pl.BlockSpec(memory_space=pl.ANY)
    smem = pl.BlockSpec(memory_space=pltpu.SMEM)
    V = pltpu.VMEM
    D = pltpu.SemaphoreType.DMA
    wide, tall = jax.ShapeDtypeStruct((OWN, RK, WD), F32), jax.ShapeDtypeStruct((OWN, RK, FW), F32)
    flat = jax.ShapeDtypeStruct((T, WD), BF16)
    outs = (
        flat, tall, tall, tall, wide,
        jax.ShapeDtypeStruct((NQ, RK, 2 * WD), BF16), jax.ShapeDtypeStruct((OWN * RK, NQ * RK), BF16),
    )
    scratch = [
        V((NS, T, WD), BF16), V((NQ,) + w.shape, BF16), V((T, WD), BF16), V((T, FW), BF16), V((T, FW), BF16),
        V((3, A, RK, WD), BF16), V((3, A, RK, FW), BF16),
        V((T, FW), F32), V((T, FW), F32), V((T, FW), BF16), V((T, FW), F32),
        V((2 * NB, 2 * RK, RB), F32), V((NS, 2 * RK, RB), F32), V((2 * NB, 2 * RK, RB), BF16),
        V((2 * NB, RK, RB), F32), V((NS, RK, RB), F32), V((2 * NB, RK, RB), BF16),
        V((NQ * RK, T), BF16), V((NQ * RK, T), BF16), V((OWN * RK, NQ * RK), BF16),
        V((NQ, RK, FW + WD), BF16), V((NQ, RK, 2 * FW), BF16), V((NQ, RK, 2 * WD), BF16),
        V((NQ, RK, FW + WD), BF16), V((NQ, RK, 2 * FW), BF16),
        V((T, WD), BF16), V((OWN, RK, WD), F32), V((3, OWN, RK, FW), F32),
        D((11,)), D((7,)), D, D((32,)), D, D((2,)), D, D((64,)), D, D, D((NS,)), D, D, D, D((NS,)), D, D((3,)), D((3,)),
    ]
    ig, gate_out, up_out, down_in, down_out, late, pick = pl.pallas_call(
        lambda *refs: kernel(dims, *refs),
        out_shape=outs,
        in_specs=[any_] * 11 + [smem] * 2,
        out_specs=tuple([any_] * 7),
        scratch_shapes=scratch,
        compiler_params=pltpu.CompilerParams(
            collective_id=0, has_side_effects=True, vmem_limit_bytes=67043328
        ),
        name="step",
    )(dy, xin, gpre, upre, w, gin, gout, uin, uout, din, dout, ids, owned)
    return pl.pallas_call(
        finish,
        out_shape=(flat, wide, tall, wide, tall, tall, wide),
        in_specs=[any_] * 7,
        out_specs=tuple([any_] * 7),
        scratch_shapes=[
            V((NQ, RK, 2 * WD), BF16), V((OWN * RK, NQ * RK), BF16),
            V((T, WD), BF16), V((3, OWN, RK, FW), F32), V((3, OWN, RK, WD), F32), D((7,)), D((7,)),
        ],
        compiler_params=pltpu.CompilerParams(vmem_limit_bytes=67043328),
        name="finish",
    )(ig, gate_out, up_out, down_in, down_out, late, pick)


def finish(
    ig_i, gout_i, uout_i, din_i, dout_i, late_i, pick_i, ig_o, gin_o, gout_o, uin_o, uout_o, din_o, dout_o,
    late, pick, ig, tall, wide, in_sem, out_sem,
):
    RK, WD = wide.shape[2:]
    loads = [(late_i, late), (pick_i, pick), (ig_i, ig)]
    loads += [(gout_i, tall.at[0]), (uout_i, tall.at[1]), (din_i, tall.at[2]), (dout_i, wide.at[0])]
    loads = [pltpu.make_async_copy(a, b, in_sem.at[i]) for i, (a, b) in enumerate(loads)]
    for cp in loads:
        cp.start()
    stores = [(wide.at[1], gin_o), (wide.at[2], uin_o), (ig, ig_o)]
    stores += [(tall.at[0], gout_o), (tall.at[1], uout_o), (tall.at[2], din_o), (wide.at[0], dout_o)]
    stores = [pltpu.make_async_copy(a, b, out_sem.at[i]) for i, (a, b) in enumerate(stores)]
    for i in range(2):
        loads[i].wait()
    d = jnp.dot(pick[...], late[...].reshape(-1, 2 * WD), preferred_element_type=F32)
    wide[1] = d[:, :WD].reshape(-1, RK, WD)
    wide[2] = d[:, WD:].reshape(-1, RK, WD)
    for i in range(2):
        stores[i].start()
    for i in range(2, 7):
        loads[i].wait()
        stores[i].start()
    for cp in stores:
        cp.wait()


def solution(mesh):
    wide = P("dp", "tensor")
    table = P(None, None, "tensor")
    owner = P("dp", None, "tensor")
    return jax.shard_map(
        shards,
        mesh=mesh,
        in_specs=(wide,) * 4 + (P("tensor", "dp"),) + (table,) * 6 + (P(), P()),
        out_specs=(wide,) + (owner,) * 6,
        check_vma=False,
    )
```

```python
import heapq

import jax
import jax.numpy as jnp
from jax import lax
from jax.experimental import pallas as pl
from jax.experimental.pallas import tpu as pltpu
from jax.sharding import PartitionSpec as P

SCALE = 2.0
F32 = jnp.float32
BF16 = jnp.bfloat16
MESH = pl.DeviceIdType.MESH
RING = 4
DEPTH = 8


def centred(a):
    return ((a + 1) % RING) - 1


def weight_hops(kind, u, v):
    sign = 1 if kind % 2 == 0 else -1
    first, second = ("x", "y") if kind < 2 else ("y", "x")
    hops = []
    if v == 0:
        if u == 0:
            hops += [(first, sign), (first, -sign)]
        elif u == -sign:
            hops += [(first, sign)]
        hops += [(second, sign), (second, -sign)]
    elif v == -sign:
        hops += [(second, sign)]
    return first, hops


def weight_timeline(unit):
    free = {(a, s): 0.0 for a in "xy" for s in (1, -1)}
    order, count = [], 0
    heap = [(0.0, k - 4, k, 0, 0) for k in range(4)]
    heapq.heapify(heap)
    while heap:
        now, _, kind, u, v = heapq.heappop(heap)
        order.append((now, kind, u, v))
        first, hops = weight_hops(kind, u, v)
        for axis, sign in hops:
            end = max(free[(axis, sign)], now) + unit
            free[(axis, sign)] = end
            nu, nv = (centred(u - sign), v) if axis == first else (u, centred(v - sign))
            heapq.heappush(heap, (end + 1.5, count, kind, nu, nv))
            count += 1
    return order


def rows_dot(a, b):
    return lax.dot_general(a, b, (((1,), (1,)), ((), ())), preferred_element_type=F32)


def turned_dot(a, b):
    return jnp.dot(a.astype(F32).T.astype(BF16), b, preferred_element_type=F32)


def kernel(
    dims,
    dy_h, x_h, gp_h, up_h, w_h, gin_h, gout_h, uin_h, uout_h, din_h, dout_h, ids, owned,
    ig_h, o_gout, o_uout, o_din, o_dout, r_i, pick_h,
    dyf, wf, xb, gp, up, tw, tf, fa, fb, hid, acc, part1, red1, res1, part2, red2, res2, big, mask, pick,
    s_d, s_o, s_i, r_d, r_o, ig, st_w, st_f,
    loc_sem, out_sem, dsend, drecv, csend, crecv, wsend, wrecv,
    rs1s, rs1r, ag1s, ag1r, rs2s, rs2r, ag2s, ag2r, a2s, a2r,
):
    NB, RB, WD, FW, NQ, NS, OWN, RK = dims
    q = lax.axis_index("dp")
    s = lax.axis_index("tensor")
    x, y = q // RING, q % RING
    z, c = s // 2, s % 2

    def dp_at(axis, sign):
        if axis == "x":
            return ((x + sign + RING) % RING) * RING + y
        return x * RING + (y + sign + RING) % RING

    def to_dp(qq):
        return {"dp": qq, "tensor": s}

    def to_tensor(ss):
        return {"dp": q, "tensor": ss}

    def z_at(off):
        return (z + off + DEPTH) % DEPTH

    def remote(src, dst, ss, rs, dev):
        return pltpu.make_async_remote_copy(
            src_ref=src, dst_ref=dst, send_sem=ss, recv_sem=rs, device_id=dev, device_id_type=MESH
        )

    loads = [
        (gp_h, gp), (up_h, up), (dy_h, dyf.at[s]), (x_h, xb), (w_h, wf.at[q]),
        (gin_h, tw.at[0]), (uin_h, tw.at[1]), (dout_h, tw.at[2]),
        (gout_h, tf.at[0]), (uout_h, tf.at[1]), (din_h, tf.at[2]),
    ]
    loads = [pltpu.make_async_copy(a, b, loc_sem.at[i]) for i, (a, b) in enumerate(loads)]

    for cp in loads[:2]:
        cp.start()

    barrier = pltpu.get_barrier_semaphore()
    peers = [to_dp(dp_at(a, sg)) for a in "xy" for sg in (1, -1)]
    peers += [to_tensor(z_at(1) * 2 + c), to_tensor(z_at(-1) * 2 + c), to_tensor(z * 2 + 1 - c)]
    for peer in peers:
        pl.semaphore_signal(barrier, inc=1, device_id=peer, device_id_type=MESH)
    pl.semaphore_wait(barrier, len(peers))

    QR = wf.shape[1] // 4
    wcount = [0]

    def wpiece(kind, u, v):
        ox, oy = (u, v) if kind < 2 else (v, u)
        qq = ((x + ox + RING) % RING) * RING + (y + oy + RING) % RING
        return wf.at[qq, pl.ds(kind * QR, QR), :]

    def wsem(kind, u, v):
        return kind * 16 + (u % RING) * RING + v % RING

    def wforward(kind, u, v):
        first, hops = weight_hops(kind, u, v)
        piece = wpiece(kind, u, v)
        src = w_h.at[pl.ds(kind * QR, QR), :] if (u, v) == (0, 0) else piece
        for axis, sign in hops:
            nu, nv = (centred(u - sign), v) if axis == first else (u, centred(v - sign))
            remote(
                src, piece, wsend, wrecv.at[wsem(kind, nu, nv)], to_dp(dp_at(axis, sign))
            ).start()
            wcount[0] += 1

    def wwait(kind, u, v):
        piece = wpiece(kind, u, v)
        remote(piece, piece, wsend, wrecv.at[wsem(kind, u, v)], to_dp(q)).wait_recv()

    HR = dyf.shape[1] // 4
    dcount = [0]
    ccount = [0]

    def dpiece(off, j, core):
        return dyf.at[z_at(off) * 2 + core, pl.ds(j * HR, HR), :]

    def dsem(off, j):
        return (off % DEPTH) * 4 + j

    def dsend_one(off, j, sign):
        piece = dpiece(off, j, c)
        src = dy_h.at[pl.ds(j * HR, HR), :] if off == 0 else piece
        remote(
            src, piece, dsend, drecv.at[dsem(off - sign, j)], to_tensor(z_at(sign) * 2 + c)
        ).start()
        dcount[0] += 1

    def dshare(off, j):
        piece = dpiece(off, j, c)
        src = dy_h.at[pl.ds(j * HR, HR), :] if off == 0 else piece
        remote(
            src, piece, csend, crecv.at[0 if j < 2 else 1 if abs(off) < 3 else 2], to_tensor(z * 2 + 1 - c)
        ).start()
        ccount[0] += 1

    lane = [(0, 0), (0, 1), (0, 2), (1, 0), (1, 1), (0, 3), (2, 0), (2, 1), (1, 2), (3, 0), (1, 3), (2, 2), (2, 3), (3, 2)]
    waiting = {sign: [(-sign * d, j if sign > 0 else j ^ 1) for d, j in lane] for sign in (1, -1)}
    held = {(0, j) for j in range(4)}

    def dflush():
        for sign in (1, -1):
            while waiting[sign] and waiting[sign][0] in held:
                dsend_one(*waiting[sign].pop(0), sign)

    def dforward(off, j):
        held.add((off, j))
        dflush()
        dshare(off, j)

    def dwait(off, j):
        piece = dpiece(off, j, c)
        remote(piece, piece, dsend, drecv.at[dsem(off, j)], to_tensor(s)).wait_recv()

    def cwait(p):
        both = dyf.at[pl.ds(0, (DEPTH, 5, DEPTH - 5)[p]), pl.ds(0, 2 * HR)]
        remote(both, both, csend, crecv.at[p], to_tensor(s)).wait_recv()

    for kind in range(4):
        wforward(kind, 0, 0)
    dflush()
    for j in range(4):
        dshare(0, j)
    for cp in loads[2:]:
        cp.start()

    outs = []

    def put(src, dst):
        cp = pltpu.make_async_copy(src, dst, out_sem.at[len(outs)])
        cp.start()
        outs.append(cp)

    ids_me = [ids[q * NB + n] for n in range(NB)]

    def rows(n):
        return pl.ds(n * RB, RB)

    def act(n):
        @pl.loop(0, RB // 16)
        def _(i):
            r = pl.ds(pl.multiple_of(n * RB + i * 16, 16), 16)
            g = gp[r, :].astype(F32)
            u = up[r, :].astype(F32)
            sg = jax.nn.sigmoid(g)
            b = g * sg
            fb[r, :] = b
            fa[r, :] = u * sg * (1.0 + g * (1.0 - sg))
            hid[r, :] = (b * u).astype(BF16)

    def ranks(n):
        a = ids_me[n]
        slab(part1, n)[...] = rows_dot(tw[0, a], xb[rows(n), :]).astype(BF16)
        slab(part1, NB + n)[...] = rows_dot(tw[1, a], xb[rows(n), :]).astype(BF16)
        slab(part1, 2 * NB + n)[...] = rows_dot(tf[2, a], hid[rows(n), :]).astype(BF16)
        slab(part1, 3 * NB + n)[...] = rows_dot(tw[2, a], dyf[s, rows(n), :]).astype(BF16)

    def picker():
        row = lax.broadcasted_iota(jnp.int32, (OWN * RK, NQ * RK), 0)
        col = lax.broadcasted_iota(jnp.int32, (OWN * RK, NQ * RK), 1)
        same = (row % RK) == (col % RK)
        rown, cown = row // RK, col // RK

        def body(qq, m):
            for o in range(OWN):
                mine = owned[q * OWN + o]
                hit = jnp.int32(0)
                for n in range(NB):
                    hit = hit + jnp.where(ids[qq * NB + n] == mine, 1, 0)
                val = jnp.where(hit > 0, 1.0, 0.0).astype(F32)
                m = m + jnp.where((cown == qq) & (rown == o) & same, 1.0, 0.0) * val
            return m

        pick[...] = lax.fori_loop(0, NQ, body, jnp.zeros((OWN * RK, NQ * RK), F32)).astype(BF16)
        put(pick, pick_h)

    def waits(a, b):
        def run():
            for cp in loads[a:b]:
                cp.wait()

        return run

    half_rows = acc.shape[0] // 2

    def multiply(k, half, fresh=False):
        r = slice(half * half_rows, (half + 1) * half_rows)
        d = rows_dot(dyf[k, r, :], wf[k])
        acc[r, :] = d if fresh else acc[r, :] + d

    def piece_at(ox, oy):
        return ((x + ox + RING) % RING) * RING + (y + oy + RING) % RING

    def near(k):
        return (k // 2 + DEPTH + 2 - z) % DEPTH < 5

    def soon(k):
        ox, oy = (k // RING + RING - x) % RING, (k % RING + RING - y) % RING
        return ((ox != 2) & (oy != 2)) | (ox + oy == 2) & (ox * oy == 0)

    def early(dz, core):
        k = z_at(dz) * 2 + core
        pl.when(soon(k))(lambda: multiply(k, 1))

    def late(ox, oy):
        k = piece_at(ox, oy)
        if abs(ox * oy) > 1:
            multiply(k, 1)
        else:
            pl.when(jnp.logical_not(near(k)))(lambda: multiply(k, 1))

    def scatter(part, red, ssem, rsem):
        def one(t, _):
            to = (s + t) % NS

            @pl.when(to < part.shape[0])
            def _():
                remote(part.at[to], red.at[s], ssem, rsem, to_tensor(to)).start()

            return 0

        lax.fori_loop(1, NS, one, 0)

    def gather_sum(part, red, res, rsem, ssem2, rsem2):
        @pl.when(s < part.shape[0])
        def _():
            others_ = red.at[pl.ds(0, NS - 1)]
            remote(others_, others_, ssem2, rsem, to_tensor(s)).wait_recv()
            red[s] = part[s]
            total = red[0].astype(F32)
            for t in range(1, NS):
                total = total + red[t].astype(F32)
            res[s] = total.astype(BF16)

            def send(t, _):
                to = (s + t) % NS
                remote(res.at[s], res.at[s], ssem2, rsem2, to_tensor(to)).start()
                return 0

            lax.fori_loop(1, NS, send, 0)

    def each_way(ref, go):
        many = ref.shape[0]
        pl.when(s < many)(lambda: go(ref.at[pl.ds(0, many - 1)]))
        pl.when(s >= many)(lambda: go(ref))

    def gather_wait(res, ssem2, rsem2):
        each_way(res, lambda r: remote(r, r, ssem2, rsem2, to_tensor(s)).wait_recv())

    def sent(part, res, ssem, ssem2):
        each_way(part, lambda r: remote(r, r, ssem, ssem, to_tensor(s)).wait_send())

        @pl.when(s < res.shape[0])
        def _():
            copies = red1.at[pl.ds(0, NS - 1), pl.ds(0, res.shape[1])]
            remote(copies, copies, ssem2, ssem2, to_tensor(s)).wait_send()

    def slab(ref, i):
        per = ref.shape[1] // RK
        return ref.at[i // per, pl.ds(i % per * RK, RK), :]

    def masks():
        def body(qq, _):
            for n in range(NB):
                hit = jnp.int32(0)
                for o in range(OWN):
                    hit = hit + jnp.where(owned[qq * OWN + o] == ids_me[n], 1, 0)
                val = jnp.where(hit > 0, 1.0, 0.0).astype(F32)
                mask[pl.ds(pl.multiple_of(qq * RK, RK), RK), n * RB : (n + 1) * RB] = jnp.full((RK, RB), val).astype(BF16)
            return 0

        lax.fori_loop(0, NQ, body, 0)

    def spread(res, base):
        row = jnp.concatenate([slab(res, base + n)[...] for n in range(NB)], axis=1)
        for qq in range(NQ):
            big[qq * RK : (qq + 1) * RK, :] = row * mask[qq * RK : (qq + 1) * RK, :]

    def packet(res, base, right, out, lo, hi, scale):
        spread(res, base)
        d = jnp.dot(big[...], right, preferred_element_type=F32)
        if scale != 1.0:
            d = d * scale
        out[:, :, lo:hi] = d.astype(BF16).reshape(NQ, RK, hi - lo)

    ring = (2, 1, -1, 0)
    others = [(a, b) for a in ring for b in ring if (a, b) != (0, 0)]
    others.sort(key=lambda o: -(abs(o[0]) + abs(o[1])))

    def peer(o, sign=1):
        return ((x + sign * o[0] + RING) % RING) * RING + (y + sign * o[1] + RING) % RING

    def exchange(g, src, dst):
        for o in others:
            to = peer(o)
            remote(src.at[to], dst.at[q], a2s.at[g], a2r.at[g], to_dp(to)).start()

    def exchanged(g, dst):
        all_ = dst.at[pl.ds(0, NQ - 1)]
        remote(all_, all_, a2s.at[g], a2r.at[g], to_dp(q)).wait_recv()

    def exchange_sent(g, src):
        all_ = src.at[pl.ds(0, NQ - 1)]
        remote(all_, all_, a2s.at[g], a2r.at[g], to_dp(q)).wait_send()

    def collect(dst, lo, hi, stage, out):
        d = jnp.dot(pick[...], dst[:, :, lo:hi].reshape(NQ * RK, hi - lo), preferred_element_type=F32)
        stage[...] = d.reshape(OWN, RK, hi - lo)
        put(stage, out)

    unit = 4.93
    events = []
    for now, kind, u, v in weight_timeline(unit):
        if (u, v) != (0, 0):
            events.append((now, "w", (kind, u, v)))
    quarter = unit * 12 / 14
    for i, (d, j) in enumerate(lane):
        for sign in (1, -1):
            events.append((3.5 + quarter * (i + 1) + (1.5 if i >= 11 else 0.0), "d", (-sign * (d + 1), j if sign > 0 else j ^ 1)))
    passed = [max(e[0] for e in events if e[1] == "d" and e[2][1] // 2 == p) for p in range(2)]
    ready = {}
    for now, what, a in events:
        if what == "w":
            o = (a[1], a[2]) if a[0] < 2 else (a[2], a[1])
            ready[o] = max(ready.get(o, 0.0), now)
    last_hop = max(e[0] for e in events if e[1] == "w" and len(weight_hops(*e[2])[1]) > 0)
    ready[(0, 0)] = 0.0

    def start_ranks():
        scatter(part1, red1, rs1s, rs1r)

    def reduce1():
        gather_sum(part1, red1, res1, rs1r, ag1s, ag1r)

    def down_packets():
        gather_wait(res1, ag1s, ag1r)
        packet(res1, 3 * NB, hid[...], s_d, 0, FW, SCALE)
        packet(res1, 2 * NB, dyf[s], s_d, FW, FW + WD, SCALE)
        r_d[q] = s_d[q]

    def down_out():
        exchange(0, s_d, r_d)

    def adapter_term(n):
        acc[rows(n), :] = acc[rows(n), :] + SCALE * turned_dot(slab(res1, 3 * NB + n)[...], tf[2, ids_me[n]])

    pieces = [(2.0, waits(0, 2))] + [(2.5 + 1.0 * n, lambda n=n: act(n)) for n in range(NB)]
    pieces += [(9.0, waits(2, 11))]
    pieces += [(11.0 + 3.0 * n, lambda n=n: ranks(n)) for n in range(NB)]
    pieces += [(29.5, picker), (32.0, masks)]
    begun = (passed[0] + 5.0, passed[1] + 3.0)
    pieces += [(begun[0], lambda: cwait(0)), (begun[1], lambda: cwait(2))]
    pieces += [(begun[0] + 0.1, start_ranks), (passed[1] + 0.1, reduce1)]
    pieces += [(last_hop + 1.4, down_packets), (last_hop + 1.5, down_out)]
    by_time = [o for o, _ in sorted(ready.items(), key=lambda kv: (kv[1], kv[0]))]
    at = begun[0] + 0.2
    for i, o in enumerate(by_time):
        at = max(at + 0.62, ready[o] + 0.1)
        pieces.append((at, lambda o=o, i=i: multiply(piece_at(*o), 0, i == 0)))
    half_near = max(e[0] for e in events if e[1] == "d" and e[2][1] > 1 and abs(e[2][0]) < 3)
    at = max(half_near + 3.0, ready[(2, 0)] + 0.5, begun[0] + 7.5)

    def clear():
        r = slice(half_rows, 2 * half_rows)
        acc[r, :] = jnp.zeros((half_rows, acc.shape[1]), F32)

    pieces += [(begun[0], clear), (at, lambda: cwait(1))]
    for dz in (0, 1, -1, 2, -2):
        for core in range(2):
            at += 0.6
            pieces.append((at, lambda dz=dz, core=core: early(dz, core)))
    at = begun[1] + 0.1
    for o in by_time:
        at = max(at + 0.3, ready[o] + 0.1)
        pieces.append((at, lambda o=o: late(*o)))
    pieces += [(last_hop + 1.6 + 0.1 * n, lambda n=n: adapter_term(n)) for n in range(NB)]

    line = [(e[0], i, e[1], e[2]) for i, e in enumerate(events)]
    line += [(t, 1000 + i, "c", f) for i, (t, f) in enumerate(pieces)]
    for _, _, what, a in sorted(line, key=lambda e: (e[0], e[1])):
        if what == "w":
            wwait(*a)
            wforward(*a)
        elif what == "d":
            dwait(*a)
            dforward(*a)
        else:
            a()

    @pl.loop(0, acc.shape[0] // 16)
    def _(i):
        r = pl.ds(pl.multiple_of(i * 16, 16), 16)
        h = acc[r, :]
        gp[r, :] = (h * fa[r, :]).astype(BF16)
        up[r, :] = (h * fb[r, :]).astype(BF16)

    for n in range(NB):
        part2[n] = SCALE * rows_dot(tf[0, ids_me[n]], gp[rows(n), :])
        part2[NB + n] = SCALE * rows_dot(tf[1, ids_me[n]], up[rows(n), :])
    scatter(part2, red2, rs2s, rs2r)
    packet(res1, 0, gp[...], s_o, 0, FW, SCALE)
    packet(res1, NB, up[...], s_o, FW, 2 * FW, SCALE)
    exchange(1, s_o, r_o)
    r_o[q] = s_o[q]
    gather_sum(part2, red2, res2, rs2r, ag2s, ag2r)
    exchanged(0, r_d)
    collect(r_d, 0, FW, st_f.at[0], o_din)
    collect(r_d, FW, FW + WD, st_w, o_dout)
    gather_wait(res2, ag2s, ag2r)
    packet(res2, 0, xb[...], s_i, 0, WD, 1.0)
    packet(res2, NB, xb[...], s_i, WD, 2 * WD, 1.0)
    exchange(2, s_i, r_i)
    put(s_i.at[q], r_i.at[q])
    for n in range(NB):
        a = ids_me[n]
        d = turned_dot(res2[n], tw[0, a]) + turned_dot(res2[NB + n], tw[1, a])
        ig[rows(n), :] = d.astype(BF16)
    put(ig, ig_h)
    exchanged(1, r_o)
    collect(r_o, 0, FW, st_f.at[1], o_gout)
    collect(r_o, FW, 2 * FW, st_f.at[2], o_uout)
    exchanged(2, r_i)

    assert wcount[0] % 4 == dcount[0] % 4 == ccount[0] % 4 == 0
    for ref, many, ss, rs in ((wf, wcount, wsend, wrecv.at[0]), (dyf, dcount, dsend, drecv.at[0]), (dyf, ccount, csend, crecv.at[0])):
        whole = ref.at[pl.ds(0, many[0] // 4)]
        remote(whole, whole, ss, rs, to_dp(q)).wait_send()
    sent(part1, res1, rs1s, ag1s)
    sent(part2, res2, rs2s, ag2s)
    exchange_sent(0, s_d)
    exchange_sent(1, s_o)
    exchange_sent(2, s_i)
    for cp in outs:
        cp.wait()


def shards(dy, xin, gpre, upre, w, gin, gout, uin, uout, din, dout, ids, owned):
    NQ, NS = lax.axis_size("dp"), lax.axis_size("tensor")
    T, WD = dy.shape
    FW = gpre.shape[1]
    A, RK = gin.shape[:2]
    NB = ids.shape[0] // NQ
    OWN = A // NQ
    RB = T // NB
    dims = (NB, RB, WD, FW, NQ, NS, OWN, RK)
    any_ = pl.BlockSpec(memory_space=pl.ANY)
    smem = pl.BlockSpec(memory_space=pltpu.SMEM)
    V = pltpu.VMEM
    D = pltpu.SemaphoreType.DMA
    wide, tall = jax.ShapeDtypeStruct((OWN, RK, WD), F32), jax.ShapeDtypeStruct((OWN, RK, FW), F32)
    flat = jax.ShapeDtypeStruct((T, WD), BF16)
    outs = (
        flat, tall, tall, tall, wide,
        jax.ShapeDtypeStruct((NQ, RK, 2 * WD), BF16), jax.ShapeDtypeStruct((OWN * RK, NQ * RK), BF16),
    )
    scratch = [
        V((NS, T, WD), BF16), V((NQ,) + w.shape, BF16), V((T, WD), BF16), V((T, FW), BF16), V((T, FW), BF16),
        V((3, A, RK, WD), BF16), V((3, A, RK, FW), BF16),
        V((T, FW), F32), V((T, FW), F32), V((T, FW), BF16), V((T, FW), F32),
        V((2 * NB, 2 * RK, RB), BF16), V((NS, 2 * RK, RB), BF16), V((2 * NB, 2 * RK, RB), BF16),
        V((2 * NB, RK, RB), F32), V((NS, RK, RB), F32), V((2 * NB, RK, RB), BF16),
        V((NQ * RK, T), BF16), V((NQ * RK, T), BF16), V((OWN * RK, NQ * RK), BF16),
        V((NQ, RK, FW + WD), BF16), V((NQ, RK, 2 * FW), BF16), V((NQ, RK, 2 * WD), BF16),
        V((NQ, RK, FW + WD), BF16), V((NQ, RK, 2 * FW), BF16),
        V((T, WD), BF16), V((OWN, RK, WD), F32), V((3, OWN, RK, FW), F32),
        D((11,)), D((7,)), D, D((32,)), D, D((3,)), D, D((64,)), D, D, D, D, D, D, D, D, D((3,)), D((3,)),
    ]
    ig, gate_out, up_out, down_in, down_out, late, pick = pl.pallas_call(
        lambda *refs: kernel(dims, *refs),
        out_shape=outs,
        in_specs=[any_] * 11 + [smem] * 2,
        out_specs=tuple([any_] * 7),
        scratch_shapes=scratch,
        compiler_params=pltpu.CompilerParams(
            collective_id=0, has_side_effects=True, vmem_limit_bytes=67043328
        ),
        name="step",
    )(dy, xin, gpre, upre, w, gin, gout, uin, uout, din, dout, ids, owned)
    return pl.pallas_call(
        finish,
        out_shape=(flat, wide, tall, wide, tall, tall, wide),
        in_specs=[any_] * 7,
        out_specs=tuple([any_] * 7),
        scratch_shapes=[
            V((NQ, RK, 2 * WD), BF16), V((OWN * RK, NQ * RK), BF16),
            V((T, WD), BF16), V((3, OWN, RK, FW), F32), V((3, OWN, RK, WD), F32), D((7,)), D((7,)),
        ],
        compiler_params=pltpu.CompilerParams(vmem_limit_bytes=67043328),
        name="finish",
    )(ig, gate_out, up_out, down_in, down_out, late, pick)


def finish(
    ig_i, gout_i, uout_i, din_i, dout_i, late_i, pick_i, ig_o, gin_o, gout_o, uin_o, uout_o, din_o, dout_o,
    late, pick, ig, tall, wide, in_sem, out_sem,
):
    RK, WD = wide.shape[2:]
    loads = [(late_i, late), (pick_i, pick), (ig_i, ig)]
    loads += [(gout_i, tall.at[0]), (uout_i, tall.at[1]), (din_i, tall.at[2]), (dout_i, wide.at[0])]
    loads = [pltpu.make_async_copy(a, b, in_sem.at[i]) for i, (a, b) in enumerate(loads)]
    for cp in loads:
        cp.start()
    stores = [(wide.at[1], gin_o), (wide.at[2], uin_o), (ig, ig_o)]
    stores += [(tall.at[0], gout_o), (tall.at[1], uout_o), (tall.at[2], din_o), (wide.at[0], dout_o)]
    stores = [pltpu.make_async_copy(a, b, out_sem.at[i]) for i, (a, b) in enumerate(stores)]
    for i in range(2):
        loads[i].wait()
    d = jnp.dot(pick[...], late[...].reshape(-1, 2 * WD), preferred_element_type=F32)
    wide[1] = d[:, :WD].reshape(-1, RK, WD)
    wide[2] = d[:, WD:].reshape(-1, RK, WD)
    for i in range(2):
        stores[i].start()
    for i in range(2, 7):
        loads[i].wait()
        stores[i].start()
    for cp in stores:
        cp.wait()


def solution(mesh):
    wide = P("dp", "tensor")
    table = P(None, None, "tensor")
    owner = P("dp", None, "tensor")
    return jax.shard_map(
        shards,
        mesh=mesh,
        in_specs=(wide,) * 4 + (P("tensor", "dp"),) + (table,) * 6 + (P(), P()),
        out_specs=(wide,) + (owner,) * 6,
        check_vma=False,
    )
```

```python
import heapq

import jax
import jax.numpy as jnp
from jax import lax
from jax.experimental import pallas as pl
from jax.experimental.pallas import tpu as pltpu
from jax.sharding import PartitionSpec as P

SCALE = 2.0
F32 = jnp.float32
BF16 = jnp.bfloat16
MESH = pl.DeviceIdType.MESH
RING = 4
DEPTH = 8


def centred(a):
    return ((a + 1) % RING) - 1


def weight_hops(kind, u, v):
    sign = 1 if kind % 2 == 0 else -1
    first, second = ("x", "y") if kind < 2 else ("y", "x")
    hops = []
    if v == 0:
        if u == 0:
            hops += [(first, sign), (first, -sign)]
        elif u == -sign:
            hops += [(first, sign)]
        hops += [(second, sign), (second, -sign)]
    elif v == -sign:
        hops += [(second, sign)]
    return first, hops


def weight_timeline(unit):
    free = {(a, s): 0.0 for a in "xy" for s in (1, -1)}
    order, count = [], 0
    heap = [(0.0, k - 4, k, 0, 0) for k in range(4)]
    heapq.heapify(heap)
    while heap:
        now, _, kind, u, v = heapq.heappop(heap)
        order.append((now, kind, u, v))
        first, hops = weight_hops(kind, u, v)
        for axis, sign in hops:
            end = max(free[(axis, sign)], now) + unit
            free[(axis, sign)] = end
            nu, nv = (centred(u - sign), v) if axis == first else (u, centred(v - sign))
            heapq.heappush(heap, (end + 1.5, count, kind, nu, nv))
            count += 1
    return order


def rows_dot(a, b):
    return lax.dot_general(a, b, (((1,), (1,)), ((), ())), preferred_element_type=F32)


def turned_dot(a, b):
    return jnp.dot(a.astype(F32).T.astype(BF16), b, preferred_element_type=F32)


def kernel(
    dims,
    dy_h, x_h, gp_h, up_h, w_h, gin_h, gout_h, uin_h, uout_h, din_h, dout_h, ids, owned,
    ig_h, o_gout, o_uout, o_din, o_dout, r_i, pick_h,
    dyf, wf, xb, gp, up, tw, tf, fa, fb, hid, acc, part1, red1, res1, part2, red2, res2, big, mask, pick,
    s_d, s_o, s_i, r_d, r_o, ig, st_w, st_f,
    loc_sem, out_sem, dsend, drecv, csend, crecv, wsend, wrecv,
    rs1s, rs1r, ag1s, ag1r, rs2s, rs2r, ag2s, ag2r, a2s, a2r,
):
    NB, RB, WD, FW, NQ, NS, OWN, RK = dims
    q = lax.axis_index("dp")
    s = lax.axis_index("tensor")
    x, y = q // RING, q % RING
    z, c = s // 2, s % 2

    def dp_at(axis, sign):
        if axis == "x":
            return ((x + sign + RING) % RING) * RING + y
        return x * RING + (y + sign + RING) % RING

    def to_dp(qq):
        return {"dp": qq, "tensor": s}

    def to_tensor(ss):
        return {"dp": q, "tensor": ss}

    def z_at(off):
        return (z + off + DEPTH) % DEPTH

    def remote(src, dst, ss, rs, dev):
        return pltpu.make_async_remote_copy(
            src_ref=src, dst_ref=dst, send_sem=ss, recv_sem=rs, device_id=dev, device_id_type=MESH
        )

    loads = [
        (gp_h, gp), (up_h, up), (dy_h, dyf.at[s]), (x_h, xb), (w_h, wf.at[q]),
        (gin_h, tw.at[0]), (uin_h, tw.at[1]), (dout_h, tw.at[2]),
        (gout_h, tf.at[0]), (uout_h, tf.at[1]), (din_h, tf.at[2]),
    ]
    loads = [pltpu.make_async_copy(a, b, loc_sem.at[i]) for i, (a, b) in enumerate(loads)]

    for cp in loads[:2]:
        cp.start()

    barrier = pltpu.get_barrier_semaphore()
    peers = [to_dp(dp_at(a, sg)) for a in "xy" for sg in (1, -1)]
    peers += [to_tensor(z_at(1) * 2 + c), to_tensor(z_at(-1) * 2 + c), to_tensor(z * 2 + 1 - c)]
    for peer in peers:
        pl.semaphore_signal(barrier, inc=1, device_id=peer, device_id_type=MESH)
    pl.semaphore_wait(barrier, len(peers))

    QR = wf.shape[1] // 4
    wcount = [0]

    def wpiece(kind, u, v):
        ox, oy = (u, v) if kind < 2 else (v, u)
        qq = ((x + ox + RING) % RING) * RING + (y + oy + RING) % RING
        return wf.at[qq, pl.ds(kind * QR, QR), :]

    def wsem(kind, u, v):
        return kind * 16 + (u % RING) * RING + v % RING

    def wforward(kind, u, v):
        first, hops = weight_hops(kind, u, v)
        piece = wpiece(kind, u, v)
        src = w_h.at[pl.ds(kind * QR, QR), :] if (u, v) == (0, 0) else piece
        for axis, sign in hops:
            nu, nv = (centred(u - sign), v) if axis == first else (u, centred(v - sign))
            remote(
                src, piece, wsend, wrecv.at[wsem(kind, nu, nv)], to_dp(dp_at(axis, sign))
            ).start()
            wcount[0] += 1

    def wwait(kind, u, v):
        piece = wpiece(kind, u, v)
        remote(piece, piece, wsend, wrecv.at[wsem(kind, u, v)], to_dp(q)).wait_recv()

    HR = dyf.shape[1] // 4
    dcount = [0]
    ccount = [0]

    def dpiece(off, j, core):
        return dyf.at[z_at(off) * 2 + core, pl.ds(j * HR, HR), :]

    def dsem(off, j):
        return (off % DEPTH) * 4 + j

    def dsend_one(off, j, sign):
        piece = dpiece(off, j, c)
        src = dy_h.at[pl.ds(j * HR, HR), :] if off == 0 else piece
        remote(
            src, piece, dsend, drecv.at[dsem(off - sign, j)], to_tensor(z_at(sign) * 2 + c)
        ).start()
        dcount[0] += 1

    def dshare(off, j):
        piece = dpiece(off, j, c)
        src = dy_h.at[pl.ds(j * HR, HR), :] if off == 0 else piece
        remote(
            src, piece, csend, crecv.at[0 if j < 2 else 1 if abs(off) < 3 else 2], to_tensor(z * 2 + 1 - c)
        ).start()
        ccount[0] += 1

    lane = [(0, 0), (0, 1), (0, 2), (1, 0), (1, 1), (0, 3), (2, 0), (2, 1), (1, 2), (3, 0), (1, 3), (2, 2), (2, 3), (3, 2)]
    waiting = {sign: [(-sign * d, j if sign > 0 else j ^ 1) for d, j in lane] for sign in (1, -1)}
    held = {(0, j) for j in range(4)}

    def dflush():
        for sign in (1, -1):
            while waiting[sign] and waiting[sign][0] in held:
                dsend_one(*waiting[sign].pop(0), sign)

    def dforward(off, j):
        held.add((off, j))
        dflush()
        dshare(off, j)

    def dwait(off, j):
        piece = dpiece(off, j, c)
        remote(piece, piece, dsend, drecv.at[dsem(off, j)], to_tensor(s)).wait_recv()

    def cwait(p):
        both = dyf.at[pl.ds(0, (DEPTH, 5, DEPTH - 5)[p]), pl.ds(0, 2 * HR)]
        remote(both, both, csend, crecv.at[p], to_tensor(s)).wait_recv()

    for kind in range(4):
        wforward(kind, 0, 0)
    dflush()
    for j in range(4):
        dshare(0, j)
    for cp in loads[2:]:
        cp.start()

    outs = []

    def put(src, dst):
        cp = pltpu.make_async_copy(src, dst, out_sem.at[len(outs)])
        cp.start()
        outs.append(cp)

    ids_me = [ids[q * NB + n] for n in range(NB)]

    def rows(n):
        return pl.ds(n * RB, RB)

    def act(n):
        @pl.loop(0, RB // 16)
        def _(i):
            r = pl.ds(pl.multiple_of(n * RB + i * 16, 16), 16)
            g = gp[r, :].astype(F32)
            u = up[r, :].astype(F32)
            sg = jax.nn.sigmoid(g)
            b = g * sg
            fb[r, :] = b
            fa[r, :] = u * sg * (1.0 + g * (1.0 - sg))
            hid[r, :] = (b * u).astype(BF16)

    def ranks(n):
        a = ids_me[n]
        slab(part1, n)[...] = rows_dot(tw[0, a], xb[rows(n), :]).astype(BF16)
        slab(part1, NB + n)[...] = rows_dot(tw[1, a], xb[rows(n), :]).astype(BF16)
        slab(part1, 2 * NB + n)[...] = rows_dot(tf[2, a], hid[rows(n), :]).astype(BF16)
        slab(part1, 3 * NB + n)[...] = rows_dot(tw[2, a], dyf[s, rows(n), :]).astype(BF16)

    def picker():
        row = lax.broadcasted_iota(jnp.int32, (OWN * RK, NQ * RK), 0)
        col = lax.broadcasted_iota(jnp.int32, (OWN * RK, NQ * RK), 1)
        same = (row % RK) == (col % RK)
        rown, cown = row // RK, col // RK

        def body(qq, m):
            for o in range(OWN):
                mine = owned[q * OWN + o]
                hit = jnp.int32(0)
                for n in range(NB):
                    hit = hit + jnp.where(ids[qq * NB + n] == mine, 1, 0)
                val = jnp.where(hit > 0, 1.0, 0.0).astype(F32)
                m = m + jnp.where((cown == qq) & (rown == o) & same, 1.0, 0.0) * val
            return m

        pick[...] = lax.fori_loop(0, NQ, body, jnp.zeros((OWN * RK, NQ * RK), F32)).astype(BF16)
        put(pick, pick_h)

    def waits(a, b):
        def run():
            for cp in loads[a:b]:
                cp.wait()

        return run

    half_rows = acc.shape[0] // 2

    def multiply(k, half, fresh=False):
        r = slice(half * half_rows, (half + 1) * half_rows)
        d = rows_dot(dyf[k, r, :], wf[k])
        acc[r, :] = d if fresh else acc[r, :] + d

    def piece_at(ox, oy):
        return ((x + ox + RING) % RING) * RING + (y + oy + RING) % RING

    def near(k):
        return (k // 2 + DEPTH + 2 - z) % DEPTH < 5

    def soon(k):
        ox, oy = (k // RING + RING - x) % RING, (k % RING + RING - y) % RING
        return ((ox != 2) & (oy != 2)) | (ox + oy == 2) & (ox * oy == 0)

    def early(dz, core):
        k = z_at(dz) * 2 + core
        pl.when(soon(k))(lambda: multiply(k, 1))

    def late(ox, oy):
        k = piece_at(ox, oy)
        if abs(ox * oy) > 1:
            multiply(k, 1)
        else:
            pl.when(jnp.logical_not(near(k)))(lambda: multiply(k, 1))

    def scatter(part, red, ssem, rsem):
        def one(t, _):
            to = (s + t) % NS

            @pl.when(to < part.shape[0])
            def _():
                remote(part.at[to], red.at[s], ssem, rsem, to_tensor(to)).start()

            return 0

        lax.fori_loop(1, NS, one, 0)

    def gather_sum(part, red, res, rsem, ssem2, rsem2):
        @pl.when(s < part.shape[0])
        def _():
            others_ = red.at[pl.ds(0, NS - 1)]
            remote(others_, others_, ssem2, rsem, to_tensor(s)).wait_recv()
            red[s] = part[s]
            total = red[0].astype(F32)
            for t in range(1, NS):
                total = total + red[t].astype(F32)
            res[s] = total.astype(BF16)

            def send(t, _):
                to = (s + t) % NS
                remote(res.at[s], res.at[s], ssem2, rsem2, to_tensor(to)).start()
                return 0

            lax.fori_loop(1, NS, send, 0)

    def each_way(ref, go):
        many = ref.shape[0]
        pl.when(s < many)(lambda: go(ref.at[pl.ds(0, many - 1)]))
        pl.when(s >= many)(lambda: go(ref))

    def gather_wait(res, ssem2, rsem2):
        each_way(res, lambda r: remote(r, r, ssem2, rsem2, to_tensor(s)).wait_recv())

    def sent(part, res, ssem, ssem2):
        each_way(part, lambda r: remote(r, r, ssem, ssem, to_tensor(s)).wait_send())

        @pl.when(s < res.shape[0])
        def _():
            copies = red1.at[pl.ds(0, NS - 1), pl.ds(0, res.shape[1])]
            remote(copies, copies, ssem2, ssem2, to_tensor(s)).wait_send()

    def slab(ref, i):
        per = ref.shape[1] // RK
        return ref.at[i // per, pl.ds(i % per * RK, RK), :]

    def masks():
        def body(qq, _):
            for n in range(NB):
                hit = jnp.int32(0)
                for o in range(OWN):
                    hit = hit + jnp.where(owned[qq * OWN + o] == ids_me[n], 1, 0)
                val = jnp.where(hit > 0, 1.0, 0.0).astype(F32)
                mask[pl.ds(pl.multiple_of(qq * RK, RK), RK), n * RB : (n + 1) * RB] = jnp.full((RK, RB), val).astype(BF16)
            return 0

        lax.fori_loop(0, NQ, body, 0)

    def spread(res, base):
        row = jnp.concatenate([slab(res, base + n)[...] for n in range(NB)], axis=1)
        for qq in range(NQ):
            big[qq * RK : (qq + 1) * RK, :] = row * mask[qq * RK : (qq + 1) * RK, :]

    def packet(res, base, right, out, lo, hi, scale):
        spread(res, base)
        d = jnp.dot(big[...], right, preferred_element_type=F32)
        if scale != 1.0:
            d = d * scale
        out[:, :, lo:hi] = d.astype(BF16).reshape(NQ, RK, hi - lo)

    ring = (2, 1, -1, 0)
    others = [(a, b) for a in ring for b in ring if (a, b) != (0, 0)]
    others.sort(key=lambda o: -(abs(o[0]) + abs(o[1])))

    def peer(o, sign=1):
        return ((x + sign * o[0] + RING) % RING) * RING + (y + sign * o[1] + RING) % RING

    def exchange(g, src, dst):
        for o in others:
            to = peer(o)
            remote(src.at[to], dst.at[q], a2s.at[g], a2r.at[g], to_dp(to)).start()

    def exchanged(g, dst):
        all_ = dst.at[pl.ds(0, NQ - 1)]
        remote(all_, all_, a2s.at[g], a2r.at[g], to_dp(q)).wait_recv()

    def exchange_sent(g, src):
        all_ = src.at[pl.ds(0, NQ - 1)]
        remote(all_, all_, a2s.at[g], a2r.at[g], to_dp(q)).wait_send()

    def collect(dst, lo, hi, stage, out):
        d = jnp.dot(pick[...], dst[:, :, lo:hi].reshape(NQ * RK, hi - lo), preferred_element_type=F32)
        stage[...] = d.reshape(OWN, RK, hi - lo)
        put(stage, out)

    unit = 4.93
    events = []
    for now, kind, u, v in weight_timeline(unit):
        if (u, v) != (0, 0):
            events.append((now, "w", (kind, u, v)))
    quarter = unit * 12 / 14
    for i, (d, j) in enumerate(lane):
        for sign in (1, -1):
            events.append((3.5 + quarter * (i + 1) + (1.5 if i >= 11 else 0.0), "d", (-sign * (d + 1), j if sign > 0 else j ^ 1)))
    passed = [max(e[0] for e in events if e[1] == "d" and e[2][1] // 2 == p) for p in range(2)]
    ready = {}
    for now, what, a in events:
        if what == "w":
            o = (a[1], a[2]) if a[0] < 2 else (a[2], a[1])
            ready[o] = max(ready.get(o, 0.0), now)
    last_hop = max(e[0] for e in events if e[1] == "w" and len(weight_hops(*e[2])[1]) > 0)
    ready[(0, 0)] = 0.0

    def start_ranks():
        scatter(part1, red1, rs1s, rs1r)

    def reduce1():
        gather_sum(part1, red1, res1, rs1r, ag1s, ag1r)

    def down_packets():
        gather_wait(res1, ag1s, ag1r)
        packet(res1, 3 * NB, hid[...], s_d, 0, FW, SCALE)
        packet(res1, 2 * NB, dyf[s], s_d, FW, FW + WD, SCALE)
        r_d[q] = s_d[q]

    def down_out():
        exchange(0, s_d, r_d)

    def adapter_term(n):
        acc[rows(n), :] = acc[rows(n), :] + SCALE * turned_dot(slab(res1, 3 * NB + n)[...], tf[2, ids_me[n]])

    pieces = [(2.0, waits(0, 2))] + [(2.5 + 1.0 * n, lambda n=n: act(n)) for n in range(NB)]
    pieces += [(9.0, waits(2, 11))]
    pieces += [(11.0 + 3.0 * n, lambda n=n: ranks(n)) for n in range(NB)]
    pieces += [(29.5, picker), (32.0, masks)]
    begun = (passed[0] + 5.0, passed[1] + 3.0)
    pieces += [(begun[0], lambda: cwait(0)), (begun[1], lambda: cwait(2))]
    pieces += [(begun[0] + 0.1, start_ranks), (passed[1] + 0.1, reduce1)]
    pieces += [(last_hop + 1.4, down_packets), (max(e[0] for e in events if e[1] == "w") + 0.01, down_out)]
    by_time = [o for o, _ in sorted(ready.items(), key=lambda kv: (kv[1], kv[0]))]
    at = begun[0] + 0.2
    for i, o in enumerate(by_time):
        at = max(at + 0.62, ready[o] + 0.1)
        pieces.append((at, lambda o=o, i=i: multiply(piece_at(*o), 0, i == 0)))
    half_near = max(e[0] for e in events if e[1] == "d" and e[2][1] > 1 and abs(e[2][0]) < 3)
    at = max(half_near + 3.0, ready[(2, 0)] + 0.5, begun[0] + 7.5)

    def clear():
        r = slice(half_rows, 2 * half_rows)
        acc[r, :] = jnp.zeros((half_rows, acc.shape[1]), F32)

    pieces += [(begun[0], clear), (at, lambda: cwait(1))]
    for dz in (0, 1, -1, 2, -2):
        for core in range(2):
            at += 0.6
            pieces.append((at, lambda dz=dz, core=core: early(dz, core)))
    at = begun[1] + 0.1
    for o in by_time:
        at = max(at + 0.3, ready[o] + 0.1)
        pieces.append((at, lambda o=o: late(*o)))
    pieces += [(last_hop + 1.6 + 0.1 * n, lambda n=n: adapter_term(n)) for n in range(NB)]

    line = [(e[0], i, e[1], e[2]) for i, e in enumerate(events)]
    line += [(t, 1000 + i, "c", f) for i, (t, f) in enumerate(pieces)]
    for _, _, what, a in sorted(line, key=lambda e: (e[0], e[1])):
        if what == "w":
            wwait(*a)
            wforward(*a)
        elif what == "d":
            dwait(*a)
            dforward(*a)
        else:
            a()

    @pl.loop(0, acc.shape[0] // 16)
    def _(i):
        r = pl.ds(pl.multiple_of(i * 16, 16), 16)
        h = acc[r, :]
        gp[r, :] = (h * fa[r, :]).astype(BF16)
        up[r, :] = (h * fb[r, :]).astype(BF16)

    for n in range(NB):
        part2[n] = SCALE * rows_dot(tf[0, ids_me[n]], gp[rows(n), :])
        part2[NB + n] = SCALE * rows_dot(tf[1, ids_me[n]], up[rows(n), :])
    scatter(part2, red2, rs2s, rs2r)
    packet(res1, 0, gp[...], s_o, 0, FW, SCALE)
    packet(res1, NB, up[...], s_o, FW, 2 * FW, SCALE)
    exchange(1, s_o, r_o)
    r_o[q] = s_o[q]
    gather_sum(part2, red2, res2, rs2r, ag2s, ag2r)
    exchanged(0, r_d)
    collect(r_d, 0, FW, st_f.at[0], o_din)
    collect(r_d, FW, FW + WD, st_w, o_dout)
    gather_wait(res2, ag2s, ag2r)
    packet(res2, 0, xb[...], s_i, 0, WD, 1.0)
    packet(res2, NB, xb[...], s_i, WD, 2 * WD, 1.0)
    exchange(2, s_i, r_i)
    put(s_i.at[q], r_i.at[q])
    for n in range(NB):
        a = ids_me[n]
        d = turned_dot(res2[n], tw[0, a]) + turned_dot(res2[NB + n], tw[1, a])
        ig[rows(n), :] = d.astype(BF16)
    put(ig, ig_h)
    exchanged(1, r_o)
    collect(r_o, 0, FW, st_f.at[1], o_gout)
    collect(r_o, FW, 2 * FW, st_f.at[2], o_uout)
    exchanged(2, r_i)

    assert wcount[0] % 4 == dcount[0] % 4 == ccount[0] % 4 == 0
    for ref, many, ss, rs in ((wf, wcount, wsend, wrecv.at[0]), (dyf, dcount, dsend, drecv.at[0]), (dyf, ccount, csend, crecv.at[0])):
        whole = ref.at[pl.ds(0, many[0] // 4)]
        remote(whole, whole, ss, rs, to_dp(q)).wait_send()
    sent(part1, res1, rs1s, ag1s)
    sent(part2, res2, rs2s, ag2s)
    exchange_sent(0, s_d)
    exchange_sent(1, s_o)
    exchange_sent(2, s_i)
    for cp in outs:
        cp.wait()


def shards(dy, xin, gpre, upre, w, gin, gout, uin, uout, din, dout, ids, owned):
    NQ, NS = lax.axis_size("dp"), lax.axis_size("tensor")
    T, WD = dy.shape
    FW = gpre.shape[1]
    A, RK = gin.shape[:2]
    NB = ids.shape[0] // NQ
    OWN = A // NQ
    RB = T // NB
    dims = (NB, RB, WD, FW, NQ, NS, OWN, RK)
    any_ = pl.BlockSpec(memory_space=pl.ANY)
    smem = pl.BlockSpec(memory_space=pltpu.SMEM)
    V = pltpu.VMEM
    D = pltpu.SemaphoreType.DMA
    wide, tall = jax.ShapeDtypeStruct((OWN, RK, WD), F32), jax.ShapeDtypeStruct((OWN, RK, FW), F32)
    flat = jax.ShapeDtypeStruct((T, WD), BF16)
    outs = (
        flat, tall, tall, tall, wide,
        jax.ShapeDtypeStruct((NQ, RK, 2 * WD), BF16), jax.ShapeDtypeStruct((OWN * RK, NQ * RK), BF16),
    )
    scratch = [
        V((NS, T, WD), BF16), V((NQ,) + w.shape, BF16), V((T, WD), BF16), V((T, FW), BF16), V((T, FW), BF16),
        V((3, A, RK, WD), BF16), V((3, A, RK, FW), BF16),
        V((T, FW), F32), V((T, FW), F32), V((T, FW), BF16), V((T, FW), F32),
        V((2 * NB, 2 * RK, RB), BF16), V((NS, 2 * RK, RB), BF16), V((2 * NB, 2 * RK, RB), BF16),
        V((2 * NB, RK, RB), F32), V((NS, RK, RB), F32), V((2 * NB, RK, RB), BF16),
        V((NQ * RK, T), BF16), V((NQ * RK, T), BF16), V((OWN * RK, NQ * RK), BF16),
        V((NQ, RK, FW + WD), BF16), V((NQ, RK, 2 * FW), BF16), V((NQ, RK, 2 * WD), BF16),
        V((NQ, RK, FW + WD), BF16), V((NQ, RK, 2 * FW), BF16),
        V((T, WD), BF16), V((OWN, RK, WD), F32), V((3, OWN, RK, FW), F32),
        D((11,)), D((7,)), D, D((32,)), D, D((3,)), D, D((64,)), D, D, D, D, D, D, D, D, D((3,)), D((3,)),
    ]
    ig, gate_out, up_out, down_in, down_out, late, pick = pl.pallas_call(
        lambda *refs: kernel(dims, *refs),
        out_shape=outs,
        in_specs=[any_] * 11 + [smem] * 2,
        out_specs=tuple([any_] * 7),
        scratch_shapes=scratch,
        compiler_params=pltpu.CompilerParams(
            collective_id=0, has_side_effects=True, vmem_limit_bytes=67043328
        ),
        name="step",
    )(dy, xin, gpre, upre, w, gin, gout, uin, uout, din, dout, ids, owned)
    return pl.pallas_call(
        finish,
        out_shape=(flat, wide, tall, wide, tall, tall, wide),
        in_specs=[any_] * 7,
        out_specs=tuple([any_] * 7),
        scratch_shapes=[
            V((NQ, RK, 2 * WD), BF16), V((OWN * RK, NQ * RK), BF16),
            V((T, WD), BF16), V((3, OWN, RK, FW), F32), V((3, OWN, RK, WD), F32), D((7,)), D((7,)),
        ],
        compiler_params=pltpu.CompilerParams(vmem_limit_bytes=67043328),
        name="finish",
    )(ig, gate_out, up_out, down_in, down_out, late, pick)


def finish(
    ig_i, gout_i, uout_i, din_i, dout_i, late_i, pick_i, ig_o, gin_o, gout_o, uin_o, uout_o, din_o, dout_o,
    late, pick, ig, tall, wide, in_sem, out_sem,
):
    RK, WD = wide.shape[2:]
    loads = [(late_i, late), (pick_i, pick), (ig_i, ig)]
    loads += [(gout_i, tall.at[0]), (uout_i, tall.at[1]), (din_i, tall.at[2]), (dout_i, wide.at[0])]
    loads = [pltpu.make_async_copy(a, b, in_sem.at[i]) for i, (a, b) in enumerate(loads)]
    for cp in loads:
        cp.start()
    stores = [(wide.at[1], gin_o), (wide.at[2], uin_o), (ig, ig_o)]
    stores += [(tall.at[0], gout_o), (tall.at[1], uout_o), (tall.at[2], din_o), (wide.at[0], dout_o)]
    stores = [pltpu.make_async_copy(a, b, out_sem.at[i]) for i, (a, b) in enumerate(stores)]
    for i in range(2):
        loads[i].wait()
    d = jnp.dot(pick[...], late[...].reshape(-1, 2 * WD), preferred_element_type=F32)
    wide[1] = d[:, :WD].reshape(-1, RK, WD)
    wide[2] = d[:, WD:].reshape(-1, RK, WD)
    for i in range(2):
        stores[i].start()
    for i in range(2, 7):
        loads[i].wait()
        stores[i].start()
    for cp in stores:
        cp.wait()


def solution(mesh):
    wide = P("dp", "tensor")
    table = P(None, None, "tensor")
    owner = P("dp", None, "tensor")
    return jax.shard_map(
        shards,
        mesh=mesh,
        in_specs=(wide,) * 4 + (P("tensor", "dp"),) + (table,) * 6 + (P(), P()),
        out_specs=(wide,) + (owner,) * 6,
        check_vma=False,
    )
```

```python
import heapq

import jax
import jax.numpy as jnp
from jax import lax
from jax.experimental import pallas as pl
from jax.experimental.pallas import tpu as pltpu
from jax.sharding import PartitionSpec as P

SCALE = 2.0
F32 = jnp.float32
BF16 = jnp.bfloat16
MESH = pl.DeviceIdType.MESH
RING = 4
DEPTH = 8


def centred(a):
    return ((a + 1) % RING) - 1


def weight_hops(kind, u, v):
    sign = 1 if kind % 2 == 0 else -1
    first, second = ("x", "y") if kind < 2 else ("y", "x")
    hops = []
    if v == 0:
        if u == 0:
            hops += [(first, sign), (first, -sign)]
        elif u == -sign:
            hops += [(first, sign)]
        hops += [(second, sign), (second, -sign)]
    elif v == -sign:
        hops += [(second, sign)]
    return first, hops


def weight_timeline(unit):
    free = {(a, s): 0.0 for a in "xy" for s in (1, -1)}
    order, count = [], 0
    heap = [(0.0, k - 4, k, 0, 0) for k in range(4)]
    heapq.heapify(heap)
    while heap:
        now, _, kind, u, v = heapq.heappop(heap)
        order.append((now, kind, u, v))
        first, hops = weight_hops(kind, u, v)
        for axis, sign in hops:
            end = max(free[(axis, sign)], now) + unit
            free[(axis, sign)] = end
            nu, nv = (centred(u - sign), v) if axis == first else (u, centred(v - sign))
            heapq.heappush(heap, (end + 1.5, count, kind, nu, nv))
            count += 1
    return order


def rows_dot(a, b):
    return lax.dot_general(a, b, (((1,), (1,)), ((), ())), preferred_element_type=F32)


def turned_dot(a, b):
    return jnp.dot(a.astype(F32).T.astype(BF16), b, preferred_element_type=F32)


def kernel(
    dims,
    dy_h, x_h, gp_h, up_h, w_h, gin_h, gout_h, uin_h, uout_h, din_h, dout_h, ids, owned,
    ig_h, o_gout, o_uout, o_din, o_dout, r_i, pick_h,
    dyf, wf, xb, gp, up, tw, tf, fa, fb, hid, acc, part1, red1, res1, part2, red2, res2, big, mask, pick,
    s_d, s_o, s_i, r_d, r_o, ig, st_w, st_f,
    loc_sem, out_sem, dsend, drecv, csend, crecv, wsend, wrecv,
    rs1s, rs1r, ag1s, ag1r, rs2s, rs2r, ag2s, ag2r, a2s, a2r,
):
    NB, RB, WD, FW, NQ, NS, OWN, RK = dims
    q = lax.axis_index("dp")
    s = lax.axis_index("tensor")
    x, y = q // RING, q % RING
    z, c = s // 2, s % 2

    def dp_at(axis, sign):
        if axis == "x":
            return ((x + sign + RING) % RING) * RING + y
        return x * RING + (y + sign + RING) % RING

    def to_dp(qq):
        return {"dp": qq, "tensor": s}

    def to_tensor(ss):
        return {"dp": q, "tensor": ss}

    def z_at(off):
        return (z + off + DEPTH) % DEPTH

    def remote(src, dst, ss, rs, dev):
        return pltpu.make_async_remote_copy(
            src_ref=src, dst_ref=dst, send_sem=ss, recv_sem=rs, device_id=dev, device_id_type=MESH
        )

    loads = [
        (gp_h, gp), (up_h, up), (dy_h, dyf.at[s]), (x_h, xb), (w_h, wf.at[q]),
        (gin_h, tw.at[0]), (uin_h, tw.at[1]), (dout_h, tw.at[2]),
        (gout_h, tf.at[0]), (uout_h, tf.at[1]), (din_h, tf.at[2]),
    ]
    loads = [pltpu.make_async_copy(a, b, loc_sem.at[i]) for i, (a, b) in enumerate(loads)]

    for cp in loads[:2]:
        cp.start()

    barrier = pltpu.get_barrier_semaphore()
    peers = [to_dp(dp_at(a, sg)) for a in "xy" for sg in (1, -1)]
    peers += [to_tensor(z_at(1) * 2 + c), to_tensor(z_at(-1) * 2 + c), to_tensor(z * 2 + 1 - c)]
    for peer in peers:
        pl.semaphore_signal(barrier, inc=1, device_id=peer, device_id_type=MESH)
    pl.semaphore_wait(barrier, len(peers))

    QR = wf.shape[1] // 4
    wcount = [0]

    def wpiece(kind, u, v):
        ox, oy = (u, v) if kind < 2 else (v, u)
        qq = ((x + ox + RING) % RING) * RING + (y + oy + RING) % RING
        return wf.at[qq, pl.ds(kind * QR, QR), :]

    def wsem(kind, u, v):
        return kind * 16 + (u % RING) * RING + v % RING

    def wforward(kind, u, v):
        first, hops = weight_hops(kind, u, v)
        piece = wpiece(kind, u, v)
        src = w_h.at[pl.ds(kind * QR, QR), :] if (u, v) == (0, 0) else piece
        for axis, sign in hops:
            nu, nv = (centred(u - sign), v) if axis == first else (u, centred(v - sign))
            remote(
                src, piece, wsend, wrecv.at[wsem(kind, nu, nv)], to_dp(dp_at(axis, sign))
            ).start()
            wcount[0] += 1

    def wwait(kind, u, v):
        piece = wpiece(kind, u, v)
        remote(piece, piece, wsend, wrecv.at[wsem(kind, u, v)], to_dp(q)).wait_recv()

    HR = dyf.shape[1] // 4
    dcount = [0]
    ccount = [0]

    def dpiece(off, j, core):
        return dyf.at[z_at(off) * 2 + core, pl.ds(j * HR, HR), :]

    def dsem(off, j):
        return (off % DEPTH) * 4 + j

    def dsend_one(off, j, sign):
        piece = dpiece(off, j, c)
        src = dy_h.at[pl.ds(j * HR, HR), :] if off == 0 else piece
        remote(
            src, piece, dsend, drecv.at[dsem(off - sign, j)], to_tensor(z_at(sign) * 2 + c)
        ).start()
        dcount[0] += 1

    def dshare(off, j):
        piece = dpiece(off, j, c)
        src = dy_h.at[pl.ds(j * HR, HR), :] if off == 0 else piece
        remote(
            src, piece, csend, crecv.at[0 if j < 2 else 1 if abs(off) < 3 else 2], to_tensor(z * 2 + 1 - c)
        ).start()
        ccount[0] += 1

    lane = [(0, 0), (0, 1), (0, 2), (1, 0), (1, 1), (0, 3), (2, 0), (2, 1), (1, 2), (3, 0), (1, 3), (2, 2), (2, 3), (3, 2)]
    waiting = {sign: [(-sign * d, j if sign > 0 else j ^ 1) for d, j in lane] for sign in (1, -1)}
    held = {(0, j) for j in range(4)}

    def dflush():
        for sign in (1, -1):
            while waiting[sign] and waiting[sign][0] in held:
                dsend_one(*waiting[sign].pop(0), sign)

    def dforward(off, j):
        held.add((off, j))
        dflush()
        dshare(off, j)

    def dwait(off, j):
        piece = dpiece(off, j, c)
        remote(piece, piece, dsend, drecv.at[dsem(off, j)], to_tensor(s)).wait_recv()

    def cwait(p):
        both = dyf.at[pl.ds(0, (DEPTH, 5, DEPTH - 5)[p]), pl.ds(0, 2 * HR)]
        remote(both, both, csend, crecv.at[p], to_tensor(s)).wait_recv()

    for kind in range(4):
        wforward(kind, 0, 0)
    dflush()
    for j in range(4):
        dshare(0, j)
    for cp in loads[2:]:
        cp.start()

    outs = []

    def put(src, dst):
        cp = pltpu.make_async_copy(src, dst, out_sem.at[len(outs)])
        cp.start()
        outs.append(cp)

    ids_me = [ids[q * NB + n] for n in range(NB)]

    def rows(n):
        return pl.ds(n * RB, RB)

    def act(n):
        @pl.loop(0, RB // 16)
        def _(i):
            r = pl.ds(pl.multiple_of(n * RB + i * 16, 16), 16)
            g = gp[r, :].astype(F32)
            u = up[r, :].astype(F32)
            sg = jax.nn.sigmoid(g)
            b = g * sg
            fb[r, :] = b
            fa[r, :] = u * sg * (1.0 + g * (1.0 - sg))
            hid[r, :] = (b * u).astype(BF16)

    def ranks(n):
        a = ids_me[n]
        slab(part1, n)[...] = rows_dot(tw[0, a], xb[rows(n), :]).astype(BF16)
        slab(part1, NB + n)[...] = rows_dot(tw[1, a], xb[rows(n), :]).astype(BF16)
        slab(part1, 2 * NB + n)[...] = rows_dot(tf[2, a], hid[rows(n), :]).astype(BF16)
        slab(part1, 3 * NB + n)[...] = rows_dot(tw[2, a], dyf[s, rows(n), :]).astype(BF16)

    def picker():
        row = lax.broadcasted_iota(jnp.int32, (OWN * RK, NQ * RK), 0)
        col = lax.broadcasted_iota(jnp.int32, (OWN * RK, NQ * RK), 1)
        same = (row % RK) == (col % RK)
        rown, cown = row // RK, col // RK

        def body(qq, m):
            for o in range(OWN):
                mine = owned[q * OWN + o]
                hit = jnp.int32(0)
                for n in range(NB):
                    hit = hit + jnp.where(ids[qq * NB + n] == mine, 1, 0)
                val = jnp.where(hit > 0, 1.0, 0.0).astype(F32)
                m = m + jnp.where((cown == qq) & (rown == o) & same, 1.0, 0.0) * val
            return m

        pick[...] = lax.fori_loop(0, NQ, body, jnp.zeros((OWN * RK, NQ * RK), F32)).astype(BF16)
        put(pick, pick_h)

    def waits(a, b):
        def run():
            for cp in loads[a:b]:
                cp.wait()

        return run

    half_rows = acc.shape[0] // 2

    def multiply(k, half, fresh=False):
        r = slice(half * half_rows, (half + 1) * half_rows)
        d = rows_dot(dyf[k, r, :], wf[k])
        acc[r, :] = d if fresh else acc[r, :] + d

    def piece_at(ox, oy):
        return ((x + ox + RING) % RING) * RING + (y + oy + RING) % RING

    def near(k):
        return (k // 2 + DEPTH + 2 - z) % DEPTH < 5

    def soon(k):
        ox, oy = (k // RING + RING - x) % RING, (k % RING + RING - y) % RING
        return ((ox != 2) & (oy != 2)) | (ox + oy == 2) & (ox * oy == 0)

    def early(dz, core):
        k = z_at(dz) * 2 + core
        pl.when(soon(k))(lambda: multiply(k, 1))

    def late(ox, oy):
        k = piece_at(ox, oy)
        if abs(ox * oy) > 1:
            multiply(k, 1)
        else:
            pl.when(jnp.logical_not(near(k)))(lambda: multiply(k, 1))

    def scatter(part, red, ssem, rsem):
        def one(t, _):
            to = (s + t) % NS

            @pl.when(to < part.shape[0])
            def _():
                remote(part.at[to], red.at[s], ssem, rsem, to_tensor(to)).start()

            return 0

        lax.fori_loop(1, NS, one, 0)

    def gather_sum(part, red, res, rsem, ssem2, rsem2):
        @pl.when(s < part.shape[0])
        def _():
            others_ = red.at[pl.ds(0, NS - 1)]
            remote(others_, others_, ssem2, rsem, to_tensor(s)).wait_recv()
            red[s] = part[s]
            total = red[0].astype(F32)
            for t in range(1, NS):
                total = total + red[t].astype(F32)
            res[s] = total.astype(BF16)

            def send(t, _):
                to = (s + t) % NS
                remote(res.at[s], res.at[s], ssem2, rsem2, to_tensor(to)).start()
                return 0

            lax.fori_loop(1, NS, send, 0)

    def each_way(ref, go):
        many = ref.shape[0]
        pl.when(s < many)(lambda: go(ref.at[pl.ds(0, many - 1)]))
        pl.when(s >= many)(lambda: go(ref))

    def gather_wait(res, ssem2, rsem2):
        each_way(res, lambda r: remote(r, r, ssem2, rsem2, to_tensor(s)).wait_recv())

    def sent(part, res, ssem, ssem2):
        each_way(part, lambda r: remote(r, r, ssem, ssem, to_tensor(s)).wait_send())

        @pl.when(s < res.shape[0])
        def _():
            copies = red1.at[pl.ds(0, NS - 1), pl.ds(0, res.shape[1])]
            remote(copies, copies, ssem2, ssem2, to_tensor(s)).wait_send()

    def slab(ref, i):
        per = ref.shape[1] // RK
        return ref.at[i // per, pl.ds(i % per * RK, RK), :]

    def masks():
        def body(qq, _):
            for n in range(NB):
                hit = jnp.int32(0)
                for o in range(OWN):
                    hit = hit + jnp.where(owned[qq * OWN + o] == ids_me[n], 1, 0)
                val = jnp.where(hit > 0, 1.0, 0.0).astype(F32)
                mask[pl.ds(pl.multiple_of(qq * RK, RK), RK), n * RB : (n + 1) * RB] = jnp.full((RK, RB), val).astype(BF16)
            return 0

        lax.fori_loop(0, NQ, body, 0)

    def spread(res, base):
        row = jnp.concatenate([slab(res, base + n)[...] for n in range(NB)], axis=1)
        for qq in range(NQ):
            big[qq * RK : (qq + 1) * RK, :] = row * mask[qq * RK : (qq + 1) * RK, :]

    def packet(res, base, right, out, lo, hi, scale):
        spread(res, base)
        d = jnp.dot(big[...], right, preferred_element_type=F32)
        if scale != 1.0:
            d = d * scale
        out[:, :, lo:hi] = d.astype(BF16).reshape(NQ, RK, hi - lo)

    ring = (2, 1, -1, 0)
    others = [(a, b) for a in ring for b in ring if (a, b) != (0, 0)]
    others.sort(key=lambda o: -(abs(o[0]) + abs(o[1])))

    def peer(o, sign=1):
        return ((x + sign * o[0] + RING) % RING) * RING + (y + sign * o[1] + RING) % RING

    def exchange(g, src, dst):
        for o in others:
            to = peer(o)
            remote(src.at[to], dst.at[q], a2s.at[g], a2r.at[g], to_dp(to)).start()

    def exchanged(g, dst):
        all_ = dst.at[pl.ds(0, NQ - 1)]
        remote(all_, all_, a2s.at[g], a2r.at[g], to_dp(q)).wait_recv()

    def exchange_sent(g, src):
        all_ = src.at[pl.ds(0, NQ - 1)]
        remote(all_, all_, a2s.at[g], a2r.at[g], to_dp(q)).wait_send()

    def collect(dst, lo, hi, stage, out):
        d = jnp.dot(pick[...], dst[:, :, lo:hi].reshape(NQ * RK, hi - lo), preferred_element_type=F32)
        stage[...] = d.reshape(OWN, RK, hi - lo)
        put(stage, out)

    unit = 4.93
    events = []
    for now, kind, u, v in weight_timeline(unit):
        if (u, v) != (0, 0):
            events.append((now, "w", (kind, u, v)))
    quarter = unit * 12 / 14
    for i, (d, j) in enumerate(lane):
        for sign in (1, -1):
            events.append((3.5 + quarter * (i + 1) + (1.5 if i >= 11 else 0.0), "d", (-sign * (d + 1), j if sign > 0 else j ^ 1)))
    passed = [max(e[0] for e in events if e[1] == "d" and e[2][1] // 2 == p) for p in range(2)]
    ready = {}
    for now, what, a in events:
        if what == "w":
            o = (a[1], a[2]) if a[0] < 2 else (a[2], a[1])
            ready[o] = max(ready.get(o, 0.0), now)
    last_hop = max(e[0] for e in events if e[1] == "w" and len(weight_hops(*e[2])[1]) > 0)
    ready[(0, 0)] = 0.0

    def start_ranks():
        scatter(part1, red1, rs1s, rs1r)

    def reduce1():
        gather_sum(part1, red1, res1, rs1r, ag1s, ag1r)

    def down_packets():
        gather_wait(res1, ag1s, ag1r)
        packet(res1, 3 * NB, hid[...], s_d, 0, FW, SCALE)
        packet(res1, 2 * NB, dyf[s], s_d, FW, FW + WD, SCALE)
        r_d[q] = s_d[q]

    def down_out():
        exchange(0, s_d, r_d)

    def adapter_term(n):
        acc[rows(n), :] = acc[rows(n), :] + SCALE * turned_dot(slab(res1, 3 * NB + n)[...], tf[2, ids_me[n]])

    pieces = [(2.0, waits(0, 2))] + [(2.5 + 1.0 * n, lambda n=n: act(n)) for n in range(NB)]
    pieces += [(9.0, waits(2, 11))]
    pieces += [(11.0 + 3.0 * n, lambda n=n: ranks(n)) for n in range(NB)]
    pieces += [(29.5, picker), (32.0, masks)]
    begun = (passed[0] + 5.0, passed[1] + 3.0)
    pieces += [(begun[0], lambda: cwait(0)), (begun[1], lambda: cwait(2))]
    pieces += [(begun[0] + 0.1, start_ranks), (passed[1] + 0.1, reduce1)]
    pieces += [(last_hop + 1.4, down_packets), (last_hop + 1.5, down_out)]
    by_time = [o for o, _ in sorted(ready.items(), key=lambda kv: (kv[1], kv[0]))]
    at = begun[0] + 0.2
    for i, o in enumerate(by_time):
        at = max(at + 0.62, ready[o] + 0.1)
        pieces.append((at, lambda o=o, i=i: multiply(piece_at(*o), 0, i == 0)))
    half_near = max(e[0] for e in events if e[1] == "d" and e[2][1] > 1 and abs(e[2][0]) < 3)
    at = max(half_near + 3.0, ready[(2, 0)] + 0.5, begun[0] + 7.5)

    def clear():
        r = slice(half_rows, 2 * half_rows)
        acc[r, :] = jnp.zeros((half_rows, acc.shape[1]), F32)

    pieces += [(begun[0], clear), (at, lambda: cwait(1))]
    for dz in (0, 1, -1, 2, -2):
        for core in range(2):
            at += 0.6
            pieces.append((at, lambda dz=dz, core=core: early(dz, core)))
    at = begun[1] + 0.1
    for o in by_time:
        at = max(at + 0.3, ready[o] + 0.1)
        pieces.append((at, lambda o=o: late(*o)))
    pieces += [(last_hop + 1.6 + 0.1 * n, lambda n=n: adapter_term(n)) for n in range(NB)]

    line = [(e[0], i, e[1], e[2]) for i, e in enumerate(events)]
    line += [(t, 1000 + i, "c", f) for i, (t, f) in enumerate(pieces)]
    for _, _, what, a in sorted(line, key=lambda e: (e[0], e[1])):
        if what == "w":
            wwait(*a)
            wforward(*a)
        elif what == "d":
            dwait(*a)
            dforward(*a)
        else:
            a()

    @pl.loop(0, acc.shape[0] // 16)
    def _(i):
        r = pl.ds(pl.multiple_of(i * 16, 16), 16)
        h = acc[r, :]
        gp[r, :] = (h * fa[r, :]).astype(BF16)
        up[r, :] = (h * fb[r, :]).astype(BF16)

    for n in range(NB):
        part2[n] = SCALE * rows_dot(tf[0, ids_me[n]], gp[rows(n), :])
        part2[NB + n] = SCALE * rows_dot(tf[1, ids_me[n]], up[rows(n), :])
    scatter(part2, red2, rs2s, rs2r)
    packet(res1, 0, gp[...], s_o, 0, FW, SCALE)
    packet(res1, NB, up[...], s_o, FW, 2 * FW, SCALE)
    exchange(1, s_o, r_o)
    r_o[q] = s_o[q]
    gather_sum(part2, red2, res2, rs2r, ag2s, ag2r)
    exchanged(0, r_d)
    collect(r_d, 0, FW, st_f.at[0], o_din)
    collect(r_d, FW, FW + WD, st_w, o_dout)
    gather_wait(res2, ag2s, ag2r)
    packet(res2, 0, xb[...], s_i, 0, WD, 1.0)
    packet(res2, NB, xb[...], s_i, WD, 2 * WD, 1.0)
    exchange(2, s_i, r_i)
    put(s_i.at[q], r_i.at[q])
    for n in range(NB):
        a = ids_me[n]
        d = turned_dot(res2[n], tw[0, a]) + turned_dot(res2[NB + n], tw[1, a])
        ig[rows(n), :] = d.astype(BF16)
    put(ig, ig_h)
    exchanged(1, r_o)
    collect(r_o, 0, FW, st_f.at[1], o_gout)
    collect(r_o, FW, 2 * FW, st_f.at[2], o_uout)
    exchanged(2, r_i)

    assert wcount[0] % 4 == dcount[0] % 4 == ccount[0] % 4 == 0
    for ref, many, ss, rs in ((wf, wcount, wsend, wrecv.at[0]), (dyf, dcount, dsend, drecv.at[0]), (dyf, ccount, csend, crecv.at[0])):
        whole = ref.at[pl.ds(0, many[0] // 4)]
        remote(whole, whole, ss, rs, to_dp(q)).wait_send()
    sent(part1, res1, rs1s, ag1s)
    sent(part2, res2, rs2s, ag2s)
    exchange_sent(0, s_d)
    exchange_sent(1, s_o)
    exchange_sent(2, s_i)
    for cp in outs:
        cp.wait()


def shards(dy, xin, gpre, upre, w, gin, gout, uin, uout, din, dout, ids, owned):
    NQ, NS = lax.axis_size("dp"), lax.axis_size("tensor")
    T, WD = dy.shape
    FW = gpre.shape[1]
    A, RK = gin.shape[:2]
    NB = ids.shape[0] // NQ
    OWN = A // NQ
    RB = T // NB
    dims = (NB, RB, WD, FW, NQ, NS, OWN, RK)
    any_ = pl.BlockSpec(memory_space=pl.ANY)
    smem = pl.BlockSpec(memory_space=pltpu.SMEM)
    V = pltpu.VMEM
    D = pltpu.SemaphoreType.DMA
    wide, tall = jax.ShapeDtypeStruct((OWN, RK, WD), F32), jax.ShapeDtypeStruct((OWN, RK, FW), F32)
    flat = jax.ShapeDtypeStruct((T, WD), BF16)
    outs = (
        flat, tall, tall, tall, wide,
        jax.ShapeDtypeStruct((NQ, RK, 2 * WD), BF16), jax.ShapeDtypeStruct((OWN * RK, NQ * RK), BF16),
    )
    scratch = [
        V((NS, T, WD), BF16), V((NQ,) + w.shape, BF16), V((T, WD), BF16), V((T, FW), BF16), V((T, FW), BF16),
        V((3, A, RK, WD), BF16), V((3, A, RK, FW), BF16),
        V((T, FW), F32), V((T, FW), F32), V((T, FW), BF16), V((T, FW), F32),
        V((2 * NB, 2 * RK, RB), BF16), V((NS, 2 * RK, RB), BF16), V((2 * NB, 2 * RK, RB), BF16),
        V((2 * NB, RK, RB), F32), V((NS, RK, RB), F32), V((2 * NB, RK, RB), BF16),
        V((NQ * RK, T), BF16), V((NQ * RK, T), BF16), V((OWN * RK, NQ * RK), BF16),
        V((NQ, RK, FW + WD), BF16), V((NQ, RK, 2 * FW), BF16), V((NQ, RK, 2 * WD), BF16),
        V((NQ, RK, FW + WD), BF16), V((NQ, RK, 2 * FW), BF16),
        V((T, WD), BF16), V((OWN, RK, WD), F32), V((3, OWN, RK, FW), F32),
        D((11,)), D((7,)), D, D((32,)), D, D((3,)), D, D((64,)), D, D, D, D, D, D, D, D, D((3,)), D((3,)),
    ]
    ig, gate_out, up_out, down_in, down_out, late, pick = pl.pallas_call(
        lambda *refs: kernel(dims, *refs),
        out_shape=outs,
        in_specs=[any_] * 11 + [smem] * 2,
        out_specs=tuple([any_] * 7),
        scratch_shapes=scratch,
        compiler_params=pltpu.CompilerParams(
            collective_id=0, has_side_effects=True, vmem_limit_bytes=67043328
        ),
        name="step",
    )(dy, xin, gpre, upre, w, gin, gout, uin, uout, din, dout, ids, owned)
    return pl.pallas_call(
        finish,
        out_shape=(flat, wide, tall, wide, tall, tall, wide),
        in_specs=[any_] * 7,
        out_specs=tuple([any_] * 7),
        scratch_shapes=[
            V((NQ, RK, 2 * WD), BF16), V((OWN * RK, NQ * RK), BF16),
            V((T, WD), BF16), V((3, OWN, RK, FW), F32), V((3, OWN, RK, WD), F32), D((7,)), D((7,)),
        ],
        compiler_params=pltpu.CompilerParams(vmem_limit_bytes=67043328),
        name="finish",
    )(ig, gate_out, up_out, down_in, down_out, late, pick)


def finish(
    ig_i, gout_i, uout_i, din_i, dout_i, late_i, pick_i, ig_o, gin_o, gout_o, uin_o, uout_o, din_o, dout_o,
    late, pick, ig, tall, wide, in_sem, out_sem,
):
    RK, WD = wide.shape[2:]
    loads = [(late_i, late), (pick_i, pick), (ig_i, ig)]
    loads += [(gout_i, tall.at[0]), (uout_i, tall.at[1]), (din_i, tall.at[2]), (dout_i, wide.at[0])]
    loads = [pltpu.make_async_copy(a, b, in_sem.at[i]) for i, (a, b) in enumerate(loads)]
    for cp in loads[2:] + loads[:2]:
        cp.start()
    stores = [(wide.at[1], gin_o), (wide.at[2], uin_o), (ig, ig_o)]
    stores += [(tall.at[0], gout_o), (tall.at[1], uout_o), (tall.at[2], din_o), (wide.at[0], dout_o)]
    stores = [pltpu.make_async_copy(a, b, out_sem.at[i]) for i, (a, b) in enumerate(stores)]
    for i in range(2, 7):
        loads[i].wait()
        stores[i].start()
    for i in range(2):
        loads[i].wait()
    d = jnp.dot(pick[...], late[...].reshape(-1, 2 * WD), preferred_element_type=F32)
    wide[1] = d[:, :WD].reshape(-1, RK, WD)
    wide[2] = d[:, WD:].reshape(-1, RK, WD)
    for i in range(2):
        stores[i].start()
    for cp in stores:
        cp.wait()


def solution(mesh):
    wide = P("dp", "tensor")
    table = P(None, None, "tensor")
    owner = P("dp", None, "tensor")
    return jax.shard_map(
        shards,
        mesh=mesh,
        in_specs=(wide,) * 4 + (P("tensor", "dp"),) + (table,) * 6 + (P(), P()),
        out_specs=(wide,) + (owner,) * 6,
        check_vma=False,
    )
```
